32 devices in a mesh: parts: 2 (over y), blk: 4 (over z), sub: 4 (over x, core).
Axes of the slice: x: 2, y: 2, z: 4, core: 2. Of those that a mesh axis runs over, the one named last changes fastest.
Arguments:
- readings: float32 [2, 24576, 256], P(None, ('parts', 'blk', 'sub')), parts along dimension 1, may hold values from -6 to 6
- coverage: int32 [2, 24576, 256], P(None, ('parts', 'blk', 'sub')), parts along dimension 1, may hold values 0 or 1
- pixel_factors: float32 [24576, 256], P(('parts', 'blk', 'sub')), parts along dimension 0, may hold values from -1.5 to 1.5
- date_factors: float32 [2048, 256], P(('parts', 'blk', 'sub')), parts along dimension 0, may hold values from -1.5 to 1.5
Outputs:
- pixel_out: float32 [24576, 256], P(('parts', 'blk', 'sub')), parts along dimension 0
- date_out: float32 [2048, 256], P(('parts', 'blk', 'sub')), parts along dimension 0
The draws below stay inside these ranges and needn't reach their ends.
There are 2 independent parts, one for each index of `parts`. The reference program is written for one: setup_inputs(seed, part) draws one part's arguments, and reference() takes and returns one part's arrays. A program takes and returns all parts, laid end to end along the dimension named above; each array names one. Nothing has to cross between parts.
All inputs are finite; a program needn't handle non-finite values. No bound on the sum of `coverage` on one device may be relied on, other than what follows from the above.
Results may differ from the reference program's by a relative error of at most 0.0001.
Values sent between devices are 32-bit elements; how exact they have to be, the bound alone decides.
No kernel may reach another device: no remote copies, remote signals or barrier semaphores. Data moves between devices by JAX's collectives and lax.ppermute only.
A program may use at most 64 MiB of HBM per device.

```python
import jax
import jax.numpy as jnp
from jax import lax

RANK = 256
DB = 256
STRATA = 2
GP = 3072
PIXELS = 12288
DATES = 1024
N_BLK = 4


def set_ends(entries, key, least, largest):
    longest = entries.shape.index(max(entries.shape))
    spots = []
    for shift in (0, 1):
        where = [jax.random.randint(jax.random.fold_in(key, axis), (), 0, length) for axis, length in enumerate(entries.shape)]
        where[longest] = (where[longest] + shift) % entries.shape[longest]
        spots.append(tuple(where))
    return entries.at[spots[0]].set(least).at[spots[1]].set(largest)


def steps_of(rng, dims, split, low, top_value):
    factor_of = 1.0
    for axis_at, shards_of in split:
        steps = jax.random.uniform(jax.random.fold_in(jax.random.fold_in(rng, 6), axis_at), (shards_of,), jnp.float32, low / len(split), top_value / len(split))
        factor_of = factor_of * jnp.repeat(jnp.exp(steps), dims[axis_at] // shards_of).reshape((-1,) + (1,) * (len(dims) - 1 - axis_at))
    return factor_of


def normal_values(key, extent, spread, bound, cuts=(), kind=jnp.bfloat16):
    level = steps_of(key, extent, cuts, -0.22, 0.18) if cuts else 1.0
    entries = jax.random.normal(key, extent, jnp.float32) * spread * level
    return jnp.minimum(jnp.maximum(entries, -bound), bound).astype(kind)


def setup_inputs(seed: int = 0, part: int = 0) -> dict:
    arg_keys = jax.random.split(jax.random.key(seed), 5)
    part_keys = jax.random.split(jax.random.fold_in(arg_keys[4], part), 5)
    readings = normal_values(part_keys[0], (STRATA, PIXELS, DB), 1.0, 6.0, ((1, 16),), jnp.float32)
    coverage = set_ends((jax.random.randint(part_keys[1], (STRATA, PIXELS, DB), 0, 5) < 3).astype(jnp.int32), jax.random.fold_in(part_keys[1], 1), 0, 1)
    pixel_factors = normal_values(part_keys[2], (PIXELS, RANK), 0.25, 1.5, ((0, 16),), jnp.float32)
    date_factors = normal_values(part_keys[3], (DATES, RANK), 0.25, 1.5, ((0, 16),), jnp.float32)
    return {"readings": readings, "coverage": coverage, "pixel_factors": pixel_factors, "date_factors": date_factors}


step_size = 0.05
ridge = 0.1
epsilon = 1e-06

def reference(readings, coverage, pixel_factors, date_factors):
    strips = pixel_factors.reshape(N_BLK, GP, RANK)
    blocks = date_factors.reshape(N_BLK, DB, RANK)
    hp = lax.Precision.HIGHEST
    for stratum in range(STRATA):
        values = readings[stratum].reshape(N_BLK, GP, DB)
        weights = coverage[stratum].reshape(N_BLK, GP, DB).astype(jnp.float32)
        predicted = jnp.einsum('gpr,gdr->gpd', strips, blocks, precision=hp)
        errors = weights * (values - predicted)
        pixel_grad = -jnp.einsum('gpd,gdr->gpr', errors, blocks, precision=hp) + ridge * strips
        date_grad = -jnp.einsum('gpd,gpr->gdr', errors, strips, precision=hp) + ridge * blocks
        pixel_ms = lax.optimization_barrier(jnp.sum(pixel_grad * pixel_grad, axis=(1, 2), keepdims=True)) / (GP * RANK)
        date_ms = lax.optimization_barrier(jnp.sum(date_grad * date_grad, axis=(1, 2), keepdims=True)) / (DB * RANK)
        strips = strips - step_size * pixel_grad / jnp.sqrt(pixel_ms + epsilon)
        blocks = blocks - step_size * date_grad / jnp.sqrt(date_ms + epsilon)
        blocks = jnp.roll(blocks, 1, axis=0)
    return (strips.reshape(PIXELS, RANK), blocks.reshape(DATES, RANK))
```

```python
import functools

import jax
import jax.numpy as jnp
from jax import lax
from jax.experimental import pallas as pl
from jax.experimental.pallas import tpu as pltpu
from jax.sharding import PartitionSpec as P

STRATA = 2

step_size = 0.05
ridge = 0.1
epsilon = 1e-06

CORES = 2
F32 = jnp.float32
BF16 = jnp.bfloat16

VMEM = pl.BlockSpec(memory_space=pltpu.VMEM)
SMEM = pl.BlockSpec(memory_space=pltpu.SMEM)

NT = (((1,), (1,)), ((), ()))
NN = (((1,), (0,)), ((), ()))
TN = (((0,), (0,)), ((), ()))


def split(value):
    high = value.astype(BF16)
    low = (value - high.astype(F32)).astype(BF16)
    return high, low


def product(a, b, dims):
    dot = functools.partial(
        lax.dot_general, dimension_numbers=dims, preferred_element_type=F32
    )
    (a_high, a_low), (b_high, b_low) = a, b
    return dot(a_high, b_high) + (dot(a_high, b_low) + dot(a_low, b_high))


def tile_squares(value):
    squares = value * value
    rows, columns = squares.shape
    folded = squares.reshape(rows // 8, 8, columns).sum(0)
    total = folded[:, :128]
    for start in range(128, columns, 128):
        total = total + folded[:, start : start + 128]
    return total


def step_of(tiles, count):
    total = tiles[0]
    for tile in tiles[1:]:
        total = total + tile
    mean = jnp.sum(total, axis=(0, 1), keepdims=True) / count
    return step_size / jnp.sqrt(mean + epsilon)


def call(kernel, outs, *args, scalars=0, flops=0):
    specs = [SMEM] * scalars + [VMEM] * (len(args) - scalars)
    size = sum(a.size * a.dtype.itemsize for a in list(args) + list(outs))
    return pl.pallas_call(
        kernel,
        out_shape=outs,
        in_specs=specs,
        out_specs=[VMEM] * len(outs),
        compiler_params=pltpu.CompilerParams(vmem_limit_bytes=16 << 20),
        cost_estimate=pl.CostEstimate(
            flops=flops, bytes_accessed=size, transcendentals=0
        ),
    )(*args)


def shape(rows, columns, dtype=F32):
    return jax.ShapeDtypeStruct((rows, columns), dtype)


def errors_and_part(place, nx, relative, values, weights, strip, block, outs):
    send_ref, keep_ref, high_ref, low_ref, part_ref = outs
    predicted = product(strip, block, NT)
    errors = weights * (values - predicted)
    errors = split(errors)
    high_ref[...], low_ref[...] = errors
    part_ref[...] = -product(errors, strip, TN)
    share = part_ref.shape[0] // (CORES * nx)
    chip, core = place
    for dx in range(nx):
        target = lax.rem(chip + dx, nx) if relative else dx
        rows = pl.ds(dx * share, share)
        for ref, owner in ((keep_ref, core), (send_ref, 1 - core)):
            start = pl.multiple_of((target * CORES + owner) * share, share)
            ref[rows, :] = part_ref[pl.ds(start, share), :]


def first_kernel(n, order, place_ref, *refs):
    shares, refs = refs[:n], refs[n:]
    values_ref, weights_ref, strip_ref = refs[:3]
    block_ref, part_ref = refs[-2], refs[-1]
    nx = n // CORES
    chip, core = place_ref[0], place_ref[1]
    share = shares[0].shape[0]
    for (dx, dc), ref in zip(order, shares):
        source = lax.rem(chip - dx + nx, nx) * CORES + lax.rem(core + dc, CORES)
        block_ref[pl.ds(pl.multiple_of(source * share, share), share), :] = ref[...]
    errors_and_part(
        (chip, core), nx, False, values_ref[...], weights_ref[...].astype(F32),
        split(strip_ref[...]), split(block_ref[...]), refs[3:7] + (part_ref,),
    )


def later_kernel(n, count, place_ref, *refs):
    own_ref, other_ref, own_block_ref, other_block_ref = refs[:4]
    values_ref, weights_ref, high_ref, low_ref = refs[4:8]
    block_ref, part_ref = refs[-2], refs[-1]
    nx = n // CORES
    chip, core = place_ref[0], place_ref[1]
    share = own_ref.shape[0] // nx
    step = step_of([tile_squares(own_ref[...]), tile_squares(other_ref[...])], count)
    for grad, block, owner in (
        (own_ref, own_block_ref, core), (other_ref, other_block_ref, 1 - core),
    ):
        updated = block[...] - step * grad[...]
        for at in range(nx):
            start = pl.multiple_of((at * CORES + owner) * share, share)
            block_ref[pl.ds(start, share), :] = updated[at * share : (at + 1) * share]
    own = pl.multiple_of((chip * CORES + core) * share, share)
    refs[12][...] = block_ref[pl.ds(own, share), :]
    errors_and_part(
        (chip, core), nx, True, values_ref[...], weights_ref[...].astype(F32),
        (high_ref[...], low_ref[...]), split(block_ref[...]), refs[8:12] + (part_ref,),
    )


def pixel_grad_kernel(high_ref, low_ref, block_ref, strip_ref, grad_ref, tile_ref):
    block = split(block_ref[...])
    grad = ridge * strip_ref[...] - product((high_ref[...], low_ref[...]), block, NN)
    grad_ref[...] = grad
    tile_ref[...] = tile_squares(grad)


def pixel_step_kernel(count, n, strip_ref, grad_ref, *refs):
    tiles, outs = refs[:n], refs[n:]
    strip = strip_ref[...] - step_of([t[...] for t in tiles], count) * grad_ref[...]
    outs[0][...] = strip
    if len(outs) > 1:
        outs[1][...], outs[2][...] = split(strip)


def gather_half_kernel(nx, place_ref, *refs):
    shares, out_ref = refs[:nx], refs[nx]
    share = shares[0].shape[0]
    for dx, ref in enumerate(shares):
        source = lax.rem(place_ref[0] - dx + nx, nx)
        out_ref[pl.ds(pl.multiple_of(source * share, share), share), :] = ref[...]


def last_grad_kernel(nx, block_ref, *refs):
    grad = ridge * block_ref[...]
    for ref in refs[:nx]:
        grad = grad + ref[...]
    refs[nx][...] = grad
    refs[nx + 1][...] = tile_squares(grad)


def on_device(readings, coverage, pixel_factors, date_factors):
    strip = pixel_factors
    pixels, rank = strip.shape
    share = date_factors.shape[0]
    n = lax.axis_size("sub")
    blocks = lax.axis_size("blk")
    nx = n // CORES
    dates = share * n
    half = share * nx
    pixel_count = pixels * n * rank
    date_count = dates * rank
    at = lax.axis_index("sub")
    place = jnp.stack([at // CORES, at % CORES]).astype(jnp.int32)
    order = [(dx, dc) for dx in range(nx) for dc in range(CORES)]

    def moved(a, dx, dc):
        return (a // CORES + dx) % nx * CORES + (a % CORES + dc) % CORES

    def within(value, dx, dc):
        return lax.ppermute(value, "sub", [(a, moved(a, dx, dc)) for a in range(n)])

    def onward(value, dx):
        pairs = [
            (b * n + a, (b + 1) % blocks * n + moved(a, dx, 0))
            for b in range(blocks) for a in range(n)
        ]
        return lax.ppermute(value, ("blk", "sub"), pairs)

    def everywhere(tile):
        return [tile] + [within(tile, *step) for step in order[1:]]

    work = 2 * pixels * dates * rank

    shares = [date_factors] + [within(date_factors, *step) for step in order[1:]]
    old = [onward(date_factors, dx) for dx in range(nx)]
    send, keep, high, low, block = call(
        functools.partial(first_kernel_out, n, order),
        [shape(half, rank), shape(half, rank), shape(pixels, dates, BF16),
         shape(pixels, dates, BF16), shape(dates, rank), shape(dates, rank)],
        place, *shares, readings[0], coverage[0], strip, scalars=1, flops=6 * work,
    )[:5]
    mine = keep + within(send, 0, 1)
    came = [onward(mine, dx) for dx in range(nx)]
    grad, tile = call(
        pixel_grad_kernel, [shape(pixels, rank), shape(8, 128)],
        high, low, block, strip, flops=3 * work,
    )
    strip, strip_high, strip_low = call(
        functools.partial(pixel_step_kernel, pixel_count, n),
        [shape(pixels, rank), shape(pixels, rank, BF16), shape(pixels, rank, BF16)],
        strip, grad, *everywhere(tile),
    )
    old_half, = call(
        functools.partial(gather_half_kernel, nx), [shape(half, rank)],
        place, *old, scalars=1,
    )
    old_other = within(old_half, 0, 1)
    date_half = sum(came[1:], came[0]) + ridge * old_half
    date_other = within(date_half, 0, 1)

    send, keep, high, low, own, block = call(
        functools.partial(later_kernel_out, n, date_count),
        [shape(half, rank), shape(half, rank), shape(pixels, dates, BF16),
         shape(pixels, dates, BF16), shape(share, rank), shape(dates, rank),
         shape(dates, rank)],
        place, date_half, date_other, old_half, old_other, readings[1], coverage[1],
        strip_high, strip_low, scalars=1, flops=6 * work,
    )[:6]
    got = within(send, 0, 1)
    came = [
        onward(keep[dx * share : (dx + 1) * share] + got[dx * share : (dx + 1) * share], dx)
        for dx in range(nx)
    ]
    old = onward(own, 0)
    grad, tile = call(
        pixel_grad_kernel, [shape(pixels, rank), shape(8, 128)],
        high, low, block, strip, flops=3 * work,
    )
    strip, = call(
        functools.partial(pixel_step_kernel, pixel_count, n), [shape(pixels, rank)],
        strip, grad, *everywhere(tile),
    )
    date_grad, tile = call(
        functools.partial(last_grad_kernel, nx), [shape(share, rank), shape(8, 128)],
        old, *came,
    )
    share_out, = call(
        functools.partial(pixel_step_kernel, date_count, n), [shape(share, rank)],
        old, date_grad, *everywhere(tile),
    )
    return strip, share_out


def first_kernel_out(n, order, *refs):
    first_kernel(n, order, *refs)


def later_kernel_out(n, count, *refs):
    later_kernel(n, count, *refs)


def solution(mesh):
    spec = P(("parts", "blk", "sub"), None)
    stacked = P(None, ("parts", "blk", "sub"), None)
    return jax.shard_map(
        on_device, mesh=mesh, in_specs=(stacked, stacked, spec, spec),
        out_specs=(spec, spec), check_vma=False,
    )
```

```python
import functools

import jax
import jax.numpy as jnp
from jax import lax
from jax.experimental import pallas as pl
from jax.experimental.pallas import tpu as pltpu
from jax.sharding import PartitionSpec as P

step_size = 0.05
ridge = 0.1
epsilon = 1e-06

CORES = 2
CHUNK = 256
F32 = jnp.float32
BF16 = jnp.bfloat16

VMEM = pl.BlockSpec(memory_space=pltpu.VMEM)
ANY = pl.BlockSpec(memory_space=pl.ANY)

NN = (((1,), (0,)), ((), ()))
TN = (((0,), (0,)), ((), ()))


def split(value):
    high = value.astype(BF16)
    low = (value - high.astype(F32)).astype(BF16)
    return high, low


def product(a, b, dims):
    dot = functools.partial(
        lax.dot_general, dimension_numbers=dims, preferred_element_type=F32
    )
    (a_high, a_low), (b_high, b_low) = a, b
    return dot(a_high, b_high) + (dot(a_high, b_low) + dot(a_low, b_high))


def tile_squares(value):
    squares = value * value
    rows, columns = squares.shape
    folded = squares.reshape(rows // 8, 8, columns).sum(0)
    total = folded[:, :128]
    for start in range(128, columns, 128):
        total = total + folded[:, start : start + 128]
    return total


def step_of(tiles, count):
    total = tiles[0]
    for tile in tiles[1:]:
        total = total + tile
    mean = jnp.sum(total, axis=(0, 1), keepdims=True) / count
    return step_size / jnp.sqrt(mean + epsilon)


def call(kernel, outs, *args, where=VMEM, scratch=(), flops=0):
    size = sum(a.size * a.dtype.itemsize for a in list(args) + list(outs))
    return pl.pallas_call(
        kernel,
        out_shape=outs,
        in_specs=[where] * len(args),
        out_specs=[VMEM] * len(outs),
        scratch_shapes=list(scratch),
        compiler_params=pltpu.CompilerParams(vmem_limit_bytes=16 << 20),
        cost_estimate=pl.CostEstimate(
            flops=flops, bytes_accessed=size, transcendentals=0
        ),
    )(*args)


def shape(rows, columns, dtype=F32):
    return jax.ShapeDtypeStruct((rows, columns), dtype)


def chunks_of(pixels):
    size = CHUNK if pixels % CHUNK == 0 else pixels
    return [pl.ds(start, size) for start in range(0, pixels, size)]


def place():
    at = lax.axis_index("sub")
    return at // CORES, lax.rem(at, CORES)


def aligned(index, size):
    return pl.ds(pl.multiple_of(index * size, size), size)


def prepare_kernel(stratum, *refs):
    with_strip = stratum == 0
    sources = refs[: 2 + with_strip]
    outs = refs[2 + with_strip : 4 + 6 * with_strip]
    buffers, sem = refs[len(sources) + len(outs) : -1], refs[-1]
    chunks = chunks_of(buffers[0].shape[0])
    copies = []
    for at, chunk in enumerate(chunks):
        row = []
        for which, (source, buffer) in enumerate(zip(sources, buffers)):
            view = source.at[chunk] if which == 2 else source.at[stratum, chunk]
            copy = pltpu.make_async_copy(view, buffer.at[chunk], sem.at[at, which])
            copy.start()
            row.append(copy)
        copies.append(row)
    for chunk, row in zip(chunks, copies):
        for copy in row:
            copy.wait()
        outs[0][:, chunk] = buffers[0][chunk, :].T
        outs[1][:, chunk] = buffers[1][chunk, :].astype(F32).T
        if with_strip:
            strip = buffers[2][chunk, :]
            outs[2][chunk, :] = strip
            outs[3][chunk, :], outs[4][chunk, :] = split(strip)
            outs[5][:, chunk], outs[6][:, chunk] = split(strip.T)


def errors_and_part(nx, relative, problem, block, outs):
    values_ref, weights_ref, th_ref, tl_ref, h_ref, l_ref = problem
    send_ref, keep_ref, high_ref, low_ref, part_ref = outs
    total = None
    for chunk in chunks_of(values_ref.shape[1]):
        predicted = product(block, (th_ref[:, chunk], tl_ref[:, chunk]), NN)
        errors = weights_ref[:, chunk] * (values_ref[:, chunk] - predicted)
        errors = split(errors)
        high_ref[:, chunk], low_ref[:, chunk] = errors
        part = product(errors, (h_ref[chunk, :], l_ref[chunk, :]), NN)
        total = part if total is None else total + part
    part_ref[...] = -total
    share = part_ref.shape[0] // (CORES * nx)
    chip, core = place()
    for dx in range(nx):
        target = lax.rem(chip + dx, nx) if relative else dx
        rows = pl.ds(dx * share, share)
        for ref, owner in ((keep_ref, core), (send_ref, 1 - core)):
            ref[rows, :] = part_ref[aligned(target * CORES + owner, share), :]


def first_kernel(order, *refs):
    n = len(order)
    nx = n // CORES
    shares, problem, outs = refs[:n], refs[n : n + 6], refs[n + 6 :]
    block_ref = outs[4]
    share = shares[0].shape[0]
    chip, core = place()
    for (dx, dc), ref in zip(order, shares):
        source = lax.rem(chip - dx + nx, nx) * CORES + lax.rem(core + dc, CORES)
        block_ref[aligned(source, share), :] = ref[...]
    errors_and_part(nx, False, problem, split(block_ref[...]), outs[:4] + outs[5:])


def later_kernel(nx, count, own_ref, other_ref, old_ref, *refs):
    problem, outs = refs[:6], refs[6:]
    share_ref, block_ref = outs[4:6]
    chip, core = place()
    share = own_ref.shape[0] // nx
    step = step_of([tile_squares(own_ref[...]), tile_squares(other_ref[...])], count)
    for grad_ref, owner in ((own_ref, core), (other_ref, 1 - core)):
        for at in range(nx):
            rows = aligned(at * CORES + owner, share)
            grad = grad_ref[pl.ds(at * share, share), :]
            block_ref[rows, :] = old_ref[rows, :] - step * grad
    share_ref[...] = block_ref[aligned(chip * CORES + core, share), :]
    errors_and_part(nx, True, problem, split(block_ref[...]), outs[:4] + outs[6:])


def gradient(strip, high, low, block):
    return ridge * strip - product((high, low), split(block), TN)


def first_gradient_kernel(nx, high_ref, low_ref, block_ref, strip_ref, *refs):
    old, (grad_ref, tile_ref, half_ref) = refs[:nx], refs[nx:]
    grad = gradient(strip_ref[...], high_ref[...], low_ref[...], block_ref[...])
    grad_ref[...] = grad
    tile_ref[...] = tile_squares(grad)
    share = old[0].shape[0]
    chip, _ = place()
    for dx, ref in enumerate(old):
        half_ref[aligned(lax.rem(chip - dx + nx, nx), share), :] = ref[...]


def later_gradient_kernel(high_ref, low_ref, block_ref, strip_ref, grad_ref, tile_ref):
    grad = gradient(strip_ref[...], high_ref[...], low_ref[...], block_ref[...])
    grad_ref[...] = grad
    tile_ref[...] = tile_squares(grad)


def first_step_kernel(count, nx, own_ref, other_ref, strip_ref, grad_ref, *refs):
    n = nx * CORES
    tiles, (strip_out, h_ref, l_ref, th_ref, tl_ref, block_ref) = refs[:n], refs[n:]
    strip = strip_ref[...] - step_of([t[...] for t in tiles], count) * grad_ref[...]
    strip_out[...] = strip
    h_ref[...], l_ref[...] = split(strip)
    th_ref[...], tl_ref[...] = split(strip.T)
    share = own_ref.shape[0] // nx
    _, core = place()
    for ref, owner in ((own_ref, core), (other_ref, 1 - core)):
        for at in range(nx):
            rows = aligned(at * CORES + owner, share)
            block_ref[rows, :] = ref[pl.ds(at * share, share), :]


def step_kernel(count, held_ref, grad_ref, *refs):
    step = step_of([t[...] for t in refs[:-1]], count)
    refs[-1][...] = held_ref[...] - step * grad_ref[...]


def last_grad_kernel(nx, block_ref, *refs):
    grad = ridge * block_ref[...]
    for ref in refs[:nx]:
        grad = grad + ref[...]
    refs[nx][...] = grad
    refs[nx + 1][...] = tile_squares(grad)


def orders(n):
    return [(dx, dc) for dx in range(n // CORES) for dc in range(CORES)]


def on_device(readings, coverage, pixel_factors, date_factors):
    pixels, rank = pixel_factors.shape
    share = date_factors.shape[0]
    n = lax.axis_size("sub")
    blocks = lax.axis_size("blk")
    nx = n // CORES
    dates = share * n
    half = share * nx
    pixel_count = pixels * n * rank
    date_count = dates * rank
    order = orders(n)
    work = 2 * pixels * dates * rank

    def moved(a, dx, dc):
        return (a // CORES + dx) % nx * CORES + (a % CORES + dc) % CORES

    def within(value, dx, dc):
        pairs = [(a, moved(a, dx, dc)) for a in range(n)]
        return lax.ppermute(value, "sub", pairs)

    def onward(value, dx):
        pairs = [
            (b * n + a, (b + 1) % blocks * n + moved(a, dx, 0))
            for b in range(blocks) for a in range(n)
        ]
        return lax.ppermute(value, ("blk", "sub"), pairs)

    def everywhere(value):
        return [value] + [within(value, *step) for step in order[1:]]

    def pixel_shape(dtype=F32):
        return shape(pixels, rank, dtype)

    def date_shape(dtype=F32):
        return shape(dates, pixels, dtype)

    def prepared(stratum, *args):
        kinds = [F32, jnp.int32, F32][: len(args)]
        outs = [date_shape(), date_shape()]
        if len(args) == 3:
            outs += [pixel_shape(), pixel_shape(BF16), pixel_shape(BF16)]
            outs += [shape(rank, pixels, BF16)] * 2
        scratch = [pltpu.VMEM((pixels, args[0].shape[2]), kind) for kind in kinds]
        scratch.append(pltpu.SemaphoreType.DMA((len(chunks_of(pixels)), len(args))))
        return call(
            functools.partial(prepare_kernel, stratum), outs, *args,
            where=ANY, scratch=scratch,
        )

    part_outs = [shape(half, rank)] * 2 + [date_shape(BF16)] * 2
    part_scratch = [pltpu.VMEM((dates, rank), F32)]

    shares = everywhere(date_factors)
    old = [onward(date_factors, dx) for dx in range(nx)]
    values, weights, strip, high, low, t_high, t_low = prepared(
        0, readings, coverage, pixel_factors
    )
    values_1, weights_1 = prepared(1, readings, coverage)
    send, keep, err_high, err_low, block = call(
        functools.partial(first_kernel, order), part_outs + [shape(dates, rank)],
        *shares, values, weights, t_high, t_low, high, low,
        scratch=part_scratch, flops=6 * work,
    )
    mine = keep + within(send, 0, 1)
    came = [onward(mine, dx) for dx in range(nx)]
    grad, tile, old_half = call(
        functools.partial(first_gradient_kernel, nx),
        [pixel_shape(), shape(8, 128), shape(half, rank)],
        err_high, err_low, block, strip, *old, flops=3 * work,
    )
    old_other = within(old_half, 0, 1)
    strip, high, low, t_high, t_low, old_block = call(
        functools.partial(first_step_kernel, pixel_count, nx),
        [pixel_shape(), pixel_shape(BF16), pixel_shape(BF16)]
        + [shape(rank, pixels, BF16)] * 2 + [shape(dates, rank)],
        old_half, old_other, strip, grad, *everywhere(tile),
    )
    date_half = sum(came[1:], came[0]) + ridge * old_half
    date_other = within(date_half, 0, 1)

    send, keep, err_high, err_low, own, block = call(
        functools.partial(later_kernel, nx, date_count),
        part_outs + [shape(share, rank), shape(dates, rank)],
        date_half, date_other, old_block, values_1, weights_1,
        t_high, t_low, high, low, scratch=part_scratch, flops=6 * work,
    )
    got = within(send, 0, 1)
    came = []
    for dx in range(nx):
        rows = slice(dx * share, (dx + 1) * share)
        came.append(onward(keep[rows] + got[rows], dx))
    held = onward(own, 0)
    grad, tile = call(
        later_gradient_kernel, [pixel_shape(), shape(8, 128)],
        err_high, err_low, block, strip, flops=3 * work,
    )
    strip, = call(
        functools.partial(step_kernel, pixel_count), [pixel_shape()],
        strip, grad, *everywhere(tile),
    )
    date_grad, tile = call(
        functools.partial(last_grad_kernel, nx),
        [shape(share, rank), shape(8, 128)], held, *came,
    )
    date_out, = call(
        functools.partial(step_kernel, date_count), [shape(share, rank)],
        held, date_grad, *everywhere(tile),
    )
    return strip, date_out


def solution(mesh):
    spec = P(("parts", "blk", "sub"), None)
    stacked = P(None, ("parts", "blk", "sub"), None)

    return jax.shard_map(
        on_device, mesh=mesh, in_specs=(stacked, stacked, spec, spec),
        out_specs=(spec, spec), check_vma=False,
    )
```

```python
import functools

import jax
import jax.numpy as jnp
from jax import lax
from jax.experimental import pallas as pl
from jax.experimental.pallas import tpu as pltpu
from jax.sharding import PartitionSpec as P


step_size = 0.05
ridge = 0.1
epsilon = 1e-06

CORES = 2
CHUNK = 256
F32 = jnp.float32
BF16 = jnp.bfloat16

VMEM = pl.BlockSpec(memory_space=pltpu.VMEM)
HBM = pl.BlockSpec(memory_space=pltpu.HBM)

NN = (((1,), (0,)), ((), ()))
TN = (((0,), (0,)), ((), ()))


def split(value):
    high = value.astype(BF16)
    low = (value - high.astype(F32)).astype(BF16)
    return high, low


def product(a, b, dims):
    dot = functools.partial(
        lax.dot_general, dimension_numbers=dims, preferred_element_type=F32
    )
    (a_high, a_low), (b_high, b_low) = a, b
    return dot(a_high, b_high) + (dot(a_high, b_low) + dot(a_low, b_high))


def tile_squares(value):
    squares = value * value
    rows, columns = squares.shape
    folded = squares.reshape(rows // 8, 8, columns).sum(0)
    total = folded[:, :128]
    for start in range(128, columns, 128):
        total = total + folded[:, start : start + 128]
    return total


def step_of(tiles, count):
    total = tiles[0]
    for tile in tiles[1:]:
        total = total + tile
    mean = jnp.sum(total, axis=(0, 1), keepdims=True) / count
    return step_size / jnp.sqrt(mean + epsilon)


def call(kernel, outs, *args, where=VMEM, scratch=(), flops=0):
    size = sum(a.size * a.dtype.itemsize for a in list(args) + list(outs))
    return pl.pallas_call(
        kernel,
        out_shape=outs,
        in_specs=[where] * len(args),
        out_specs=[VMEM] * len(outs),
        scratch_shapes=list(scratch),
        compiler_params=pltpu.CompilerParams(vmem_limit_bytes=16 << 20),
        cost_estimate=pl.CostEstimate(
            flops=flops, bytes_accessed=size, transcendentals=0
        ),
    )(*args)


def shape(rows, columns, dtype=F32):
    return jax.ShapeDtypeStruct((rows, columns), dtype)


def chunks_of(pixels):
    size = CHUNK if pixels % CHUNK == 0 else pixels
    return [pl.ds(start, size) for start in range(0, pixels, size)]


def place():
    at = lax.axis_index("sub")
    return at // CORES, lax.rem(at, CORES)


def aligned(index, size):
    return pl.ds(pl.multiple_of(index * size, size), size)


def prepare_kernel(stratum, share, *refs):
    with_strip = stratum == 0
    sources = refs[: 2 + with_strip]
    outs = refs[2 + with_strip : 4 + 6 * with_strip]
    buffers, sem = refs[len(sources) + len(outs) : -1], refs[-1]
    pixels, dates = buffers[0].shape
    nx = dates // share // CORES
    chunks = chunks_of(pixels)
    copies = []
    for at, chunk in enumerate(chunks):
        row = []
        for which, (source, buffer) in enumerate(zip(sources, buffers)):
            view = source.at[chunk] if which == 2 else source.at[stratum, chunk]
            copy = pltpu.make_async_copy(view, buffer.at[chunk], sem.at[at, which])
            copy.start()
            row.append(copy)
        copies.append(row)
    _, core = place()
    for chunk, row in zip(chunks, copies):
        for copy in row:
            copy.wait()
        for out, buffer in zip(outs[:2], buffers[:2]):
            turned = buffer[chunk, :].astype(F32).T
            for at in range(nx * CORES):
                own = jnp.where(core == at % CORES, nx, 0)
                rows = aligned(own + at // CORES, share)
                out[rows, chunk] = turned[at * share : (at + 1) * share]
        if with_strip:
            strip = buffers[2][chunk, :]
            outs[2][chunk, :] = strip
            outs[3][chunk, :], outs[4][chunk, :] = split(strip)
            outs[5][:, chunk], outs[6][:, chunk] = split(strip.T)


def errors_and_part(side, problem, block, high_ref, low_ref):
    values_ref, weights_ref, th_ref, tl_ref, h_ref, l_ref = problem
    half = block.shape[0]
    rows = slice(side * half, (side + 1) * half)
    block = split(block)
    total = None
    for chunk in chunks_of(values_ref.shape[1]):
        predicted = product(block, (th_ref[:, chunk], tl_ref[:, chunk]), NN)
        errors = weights_ref[rows, chunk] * (values_ref[rows, chunk] - predicted)
        errors = split(errors)
        high_ref[:, chunk], low_ref[:, chunk] = errors
        part = product(errors, (h_ref[chunk, :], l_ref[chunk, :]), NN)
        total = part if total is None else total + part
    return -total


def with_ridge(part, block):
    chip, _ = place()
    return part + jnp.where(chip == 0, ridge, 0.0) * block


def first_send_kernel(order, *refs):
    n = len(order)
    nx = n // CORES
    shares, problem = refs[:n], refs[n : n + 6]
    send_ref, high_ref, low_ref, other_ref, own_ref = refs[n + 6 :]
    share = shares[0].shape[0]
    chip, _ = place()
    for (dx, dc), ref in zip(order, shares):
        rows = aligned(lax.rem(chip - dx + nx, nx), share)
        (other_ref if dc else own_ref)[rows, :] = ref[...]
    send_ref[...] = errors_and_part(0, problem, other_ref[...], high_ref, low_ref)


def first_keep_kernel(block_ref, *refs):
    problem, (keep_ref, high_ref, low_ref) = refs[:6], refs[6:]
    block = block_ref[...]
    part = errors_and_part(1, problem, block, high_ref, low_ref)
    keep_ref[...] = with_ridge(part, block)


def later_step(count, own_ref, other_ref):
    return step_of([tile_squares(own_ref[...]), tile_squares(other_ref[...])], count)


def later_send_kernel(count, own_ref, other_ref, message_ref, *refs):
    problem, (send_ref, high_ref, low_ref, block_ref) = refs[:6], refs[6:]
    step = later_step(count, own_ref, other_ref)
    block = message_ref[: other_ref.shape[0], :] - step * other_ref[...]
    block_ref[...] = block
    send_ref[...] = errors_and_part(0, problem, block, high_ref, low_ref)


def later_keep_kernel(count, share, own_ref, other_ref, message_ref, *refs):
    problem, (keep_ref, high_ref, low_ref, block_ref, share_ref) = refs[:6], refs[6:]
    step = later_step(count, own_ref, other_ref)
    block = message_ref[: own_ref.shape[0], :] - step * own_ref[...]
    block_ref[...] = block
    chip, _ = place()
    share_ref[...] = block_ref[aligned(chip, share), :]
    part = errors_and_part(1, problem, block, high_ref, low_ref)
    keep_ref[...] = with_ridge(part, block)


def pixel_gradient(strip_ref, errors, blocks):
    joined = [jnp.concatenate([ref[...] for ref in part], 0) for part in errors]
    block = jnp.concatenate([ref[...] for ref in blocks], 0)
    return ridge * strip_ref[...] - product(joined, split(block), TN)


def first_gradient_kernel(strip_ref, old_ref, h0, l0, h1, l1, b0, b1, grad_ref, out_ref):
    grad = pixel_gradient(strip_ref, ((h0, h1), (l0, l1)), (b0, b1))
    grad_ref[...] = grad
    share, rank = old_ref.shape
    out_ref[:share, :] = old_ref[...]
    out_ref[share:, :128] = tile_squares(grad)
    if rank > 128:
        out_ref[share:, 128:] = jnp.zeros((8, rank - 128), F32)


def later_gradient_kernel(strip_ref, h0, l0, h1, l1, b0, b1, grad_ref, tile_ref):
    grad = pixel_gradient(strip_ref, ((h0, h1), (l0, l1)), (b0, b1))
    grad_ref[...] = grad
    tile_ref[...] = tile_squares(grad)


def join_kernel(*refs):
    messages, out_ref = refs[:-1], refs[-1]
    nx = len(messages)
    share = messages[0].shape[0] - 8
    chip, _ = place()
    total = None
    for dx, ref in enumerate(messages):
        out_ref[aligned(lax.rem(chip - dx + nx, nx), share), :] = ref[:share, :]
        tile = ref[share:, :]
        total = tile if total is None else total + tile
    out_ref[nx * share :, :] = total


def first_step_kernel(count, own_ref, other_ref, strip_ref, grad_ref, *outs):
    strip_out, h_ref, l_ref, th_ref, tl_ref = outs
    half = own_ref.shape[0] - 8
    step = step_of([own_ref[half:, :128], other_ref[half:, :128]], count)
    strip = strip_ref[...] - step * grad_ref[...]
    strip_out[...] = strip
    h_ref[...], l_ref[...] = split(strip)
    th_ref[...], tl_ref[...] = split(strip.T)


def step_kernel(count, held_ref, grad_ref, *refs):
    step = step_of([t[...] for t in refs[:-1]], count)
    refs[-1][...] = held_ref[...] - step * grad_ref[...]


def last_gradient_kernel(share, *refs):
    parts, (grad_ref, tile_ref), sum_ref = refs[:-3], refs[-3:-1], refs[-1]
    total = parts[0][...]
    for ref in parts[1:]:
        total = total + ref[...]
    sum_ref[...] = total
    tile_ref[...] = tile_squares(total)
    chip, _ = place()
    grad_ref[...] = sum_ref[aligned(chip, share), :]


def orders(n):
    return [(dx, dc) for dx in range(n // CORES) for dc in range(CORES)]


def on_device(readings, coverage, pixel_factors, date_factors):
    pixels, rank = pixel_factors.shape
    share = date_factors.shape[0]
    n = lax.axis_size("sub")
    blocks = lax.axis_size("blk")
    nx = n // CORES
    dates = share * n
    half = share * nx
    pixel_count = pixels * n * rank
    date_count = dates * rank
    order = orders(n)
    work = pixels * dates * rank

    def moved(a, dx, dc):
        return (a // CORES + dx) % nx * CORES + (a % CORES + dc) % CORES

    def within(value, dx, dc):
        pairs = [(a, moved(a, dx, dc)) for a in range(n)]
        return lax.ppermute(value, "sub", pairs)

    def onward(value, dx):
        pairs = [
            (b * n + a, (b + 1) % blocks * n + moved(a, dx, 0))
            for b in range(blocks) for a in range(n)
        ]
        return lax.ppermute(value, ("blk", "sub"), pairs)

    def chips(value):
        return [value] + [within(value, dx, 0) for dx in range(1, nx)]

    strip_shapes = [shape(pixels, rank)] + [shape(pixels, rank, BF16)] * 2
    strip_shapes += [shape(rank, pixels, BF16)] * 2
    part_shapes = [shape(half, rank)] + [shape(half, pixels, BF16)] * 2

    def prepared(stratum, *args):
        kinds = [F32, jnp.int32, F32][: len(args)]
        outs = [shape(dates, pixels)] * 2
        if len(args) == 3:
            outs += strip_shapes
        scratch = [pltpu.VMEM((pixels, args[0].shape[2]), kind) for kind in kinds]
        scratch.append(pltpu.SemaphoreType.DMA((len(chunks_of(pixels)), len(args))))
        return call(
            functools.partial(prepare_kernel, stratum, share), outs, *args,
            where=HBM, scratch=scratch,
        )

    shares = [date_factors]
    shares += [within(date_factors, *step) for step in order[1:]]
    old = onward(date_factors, 0)
    values, weights, strip, *halves = prepared(0, readings, coverage, pixel_factors)
    values_1, weights_1 = prepared(1, readings, coverage)
    problem = (values, weights, halves[2], halves[3], halves[0], halves[1])
    send, h0, l0, b0, b1 = call(
        functools.partial(first_send_kernel, order),
        part_shapes + [shape(half, rank)] * 2, *shares, *problem, flops=6 * work,
    )
    got = within(send, 0, 1)
    keep, h1, l1 = call(first_keep_kernel, part_shapes, b1, *problem, flops=6 * work)
    mine = keep + got
    came = [onward(mine, dx) for dx in range(nx)]
    grad, message = call(
        first_gradient_kernel, [shape(pixels, rank), shape(share + 8, rank)],
        strip, old, h0, l0, h1, l1, b0, b1, flops=6 * work,
    )
    messages = chips(message)
    own_message, = call(join_kernel, [shape(half + 8, rank)], *messages)
    other_message = within(own_message, 0, 1)
    strip, *halves = call(
        functools.partial(first_step_kernel, pixel_count), strip_shapes,
        own_message, other_message, strip, grad,
    )
    own_grad = sum(came[1:], came[0])
    other_grad = within(own_grad, 0, 1)

    problem = (values_1, weights_1, halves[2], halves[3], halves[0], halves[1])
    send, h0, l0, b0 = call(
        functools.partial(later_send_kernel, date_count),
        part_shapes + [shape(half, rank)],
        own_grad, other_grad, other_message, *problem, flops=6 * work,
    )
    got = within(send, 0, 1)
    keep, h1, l1, b1, own = call(
        functools.partial(later_keep_kernel, date_count, share),
        part_shapes + [shape(half, rank), shape(share, rank)],
        own_grad, other_grad, own_message, *problem, flops=6 * work,
    )
    mine = keep + got
    came = [onward(mine, dx) for dx in range(nx)]
    held = onward(own, 0)
    grad, tile = call(
        later_gradient_kernel, [shape(pixels, rank), shape(8, 128)],
        strip, h0, l0, h1, l1, b0, b1, flops=6 * work,
    )
    tiles = chips(tile)
    tile = sum(tiles[1:], tiles[0])
    strip, = call(
        functools.partial(step_kernel, pixel_count), [shape(pixels, rank)],
        strip, grad, tile, within(tile, 0, 1),
    )
    date_grad, tile = call(
        functools.partial(last_gradient_kernel, share),
        [shape(share, rank), shape(8, 128)], *came,
        scratch=[pltpu.VMEM((half, rank), F32)],
    )
    date_out, = call(
        functools.partial(step_kernel, date_count), [shape(share, rank)],
        held, date_grad, tile, within(tile, 0, 1),
    )
    return strip, date_out


def solution(mesh):
    spec = P(("parts", "blk", "sub"), None)
    stacked = P(None, ("parts", "blk", "sub"), None)

    return jax.shard_map(
        on_device, mesh=mesh, in_specs=(stacked, stacked, spec, spec),
        out_specs=(spec, spec), check_vma=False,
    )
```

```python
import functools

import jax
import jax.numpy as jnp
from jax import lax
from jax.experimental import pallas as pl
from jax.experimental.pallas import tpu as pltpu
from jax.sharding import PartitionSpec as P


step_size = 0.05
ridge = 0.1
epsilon = 1e-06

CORES = 2
CHUNK = 256
HIDDEN = 1e9
GRANT = 16 << 20
WIDE = 54_000_000
F32 = jnp.float32
BF16 = jnp.bfloat16

VMEM = pl.BlockSpec(memory_space=pltpu.VMEM)
HBM = pl.BlockSpec(memory_space=pltpu.HBM)

NT = (((1,), (1,)), ((), ()))
NN = (((1,), (0,)), ((), ()))
TN = (((0,), (0,)), ((), ()))


def split(value):
    high = value.astype(BF16)
    low = (value - high.astype(F32)).astype(BF16)
    return high, low


def product(a, b, dims):
    dot = functools.partial(
        lax.dot_general, dimension_numbers=dims, preferred_element_type=F32
    )
    (a_high, a_low), (b_high, b_low) = a, b
    return dot(a_high, b_high) + (dot(a_high, b_low) + dot(a_low, b_high))


def tile_squares(value):
    squares = value * value
    rows, columns = squares.shape
    folded = squares.reshape(rows // 8, 8, columns).sum(0)
    total = folded[:, :128]
    for start in range(128, columns, 128):
        total = total + folded[:, start : start + 128]
    return total


def step_of(tiles, count):
    total = tiles[0]
    for tile in tiles[1:]:
        total = total + tile
    mean = jnp.sum(total, axis=(0, 1), keepdims=True) / count
    return step_size / jnp.sqrt(mean + epsilon)


def call(kernel, outs, *args, where=VMEM, scratch=(), flops=0, grant=GRANT):
    size = sum(a.size * a.dtype.itemsize for a in list(args) + list(outs))
    return pl.pallas_call(
        kernel,
        out_shape=outs,
        in_specs=[where] * len(args),
        out_specs=[VMEM] * len(outs),
        scratch_shapes=list(scratch),
        compiler_params=pltpu.CompilerParams(vmem_limit_bytes=grant),
        cost_estimate=pl.CostEstimate(
            flops=flops, bytes_accessed=size, transcendentals=0
        ),
    )(*args)


def shape(rows, columns, dtype=F32):
    return jax.ShapeDtypeStruct((rows, columns), dtype)


def chunks_of(pixels):
    size = CHUNK if pixels % CHUNK == 0 else pixels
    return [pl.ds(start, size) for start in range(0, pixels, size)]


def place():
    at = lax.axis_index("sub")
    return at // CORES, lax.rem(at, CORES)


def aligned(index, size):
    return pl.ds(pl.multiple_of(index * size, size), size)


def prepare_kernel(stratum, share, *refs):
    with_strip = stratum == 0
    sources = refs[: 2 + with_strip]
    outs = refs[len(sources) : len(sources) + 1 + 3 * with_strip]
    buffers, sem = refs[len(sources) + len(outs) : -1], refs[-1]
    pixels, dates = buffers[0].shape
    nx = dates // share // CORES
    chunks = chunks_of(pixels)
    copies = []
    for at, chunk in enumerate(chunks):
        row = []
        for which, (source, buffer) in enumerate(zip(sources, buffers)):
            view = source.at[chunk] if which == 2 else source.at[stratum, chunk]
            copy = pltpu.make_async_copy(view, buffer.at[chunk], sem.at[at, which])
            copy.start()
            row.append(copy)
        copies.append(row)
    _, core = place()
    for chunk, row in zip(chunks, copies):
        for copy in row:
            copy.wait()
        seen = jnp.where(buffers[1][chunk, :] != 0, buffers[0][chunk, :], HIDDEN)
        turned = seen.T
        for at in range(nx * CORES):
            own = jnp.where(core == at % CORES, nx, 0)
            rows = aligned(own + at // CORES, share)
            outs[0][rows, chunk] = turned[at * share : (at + 1) * share]
        if with_strip:
            strip = buffers[2][chunk, :]
            outs[1][chunk, :] = strip
            outs[2][chunk, :], outs[3][chunk, :] = split(strip)


def errors_and_part(side, problem, block, high_ref, low_ref):
    values_ref, h_ref, l_ref = problem
    half = block.shape[0]
    rows = slice(side * half, (side + 1) * half)
    block = split(block)
    total = None
    for chunk in chunks_of(values_ref.shape[1]):
        strip = (h_ref[chunk, :], l_ref[chunk, :])
        values = values_ref[rows, chunk]
        errors = jnp.where(values < HIDDEN, values - product(block, strip, NT), 0.0)
        errors = split(errors)
        high_ref[:, chunk], low_ref[:, chunk] = errors
        part = product(errors, strip, NN)
        total = part if total is None else total + part
    return -total


def with_ridge(part, block):
    chip, _ = place()
    return part + jnp.where(chip == 0, ridge, 0.0) * block


def assemble(shares, block_ref):
    nx = len(shares)
    share = shares[0].shape[0]
    chip, _ = place()
    for dx, ref in enumerate(shares):
        block_ref[aligned(lax.rem(chip - dx + nx, nx), share), :] = ref[...]


def first_send_kernel(nx, *refs):
    problem, (send_ref, high_ref, low_ref, block_ref) = refs[nx : nx + 3], refs[nx + 3 :]
    assemble(refs[:nx], block_ref)
    send_ref[...] = errors_and_part(0, problem, block_ref[...], high_ref, low_ref)


def first_keep_kernel(nx, *refs):
    problem, (keep_ref, high_ref, low_ref, block_ref) = refs[nx : nx + 3], refs[nx + 3 :]
    assemble(refs[:nx], block_ref)
    block = block_ref[...]
    part = errors_and_part(1, problem, block, high_ref, low_ref)
    keep_ref[...] = with_ridge(part, block)


def later_step(count, own_ref, other_ref):
    return step_of([tile_squares(own_ref[...]), tile_squares(other_ref[...])], count)


def later_send_kernel(count, own_ref, other_ref, message_ref, *refs):
    problem, (send_ref, high_ref, low_ref, block_ref) = refs[:3], refs[3:]
    step = later_step(count, own_ref, other_ref)
    block = message_ref[: other_ref.shape[0], :] - step * other_ref[...]
    block_ref[...] = block
    send_ref[...] = errors_and_part(0, problem, block, high_ref, low_ref)


def later_keep_kernel(count, share, own_ref, other_ref, message_ref, *refs):
    problem, (keep_ref, high_ref, low_ref, block_ref, share_ref) = refs[:3], refs[3:]
    step = later_step(count, own_ref, other_ref)
    block = message_ref[: own_ref.shape[0], :] - step * own_ref[...]
    block_ref[...] = block
    chip, _ = place()
    share_ref[...] = block_ref[aligned(chip, share), :]
    part = errors_and_part(1, problem, block, high_ref, low_ref)
    keep_ref[...] = with_ridge(part, block)


def pixel_gradient(strip_ref, errors, blocks):
    joined = [jnp.concatenate([ref[...] for ref in part], 0) for part in errors]
    block = jnp.concatenate([ref[...] for ref in blocks], 0)
    return ridge * strip_ref[...] - product(joined, split(block), TN)


def gradient_kernel(strip_ref, h0, l0, h1, l1, b0, b1, grad_ref, tile_ref):
    grad = pixel_gradient(strip_ref, ((h0, h1), (l0, l1)), (b0, b1))
    grad_ref[...] = grad
    tile = tile_squares(grad)
    columns = tile_ref.shape[1]
    tile_ref[:, :128] = tile
    if columns > 128:
        tile_ref[:, 128:] = jnp.zeros((8, columns - 128), F32)


def join_kernel(*refs):
    messages, out_ref = refs[:-1], refs[-1]
    nx = len(messages)
    share = messages[0].shape[0] - 8
    chip, _ = place()
    total = None
    for dx, ref in enumerate(messages):
        out_ref[aligned(lax.rem(chip - dx + nx, nx), share), :] = ref[:share, :]
        tile = ref[share:, :]
        total = tile if total is None else total + tile
    out_ref[nx * share :, :] = total


def first_step_kernel(count, own_ref, other_ref, strip_ref, grad_ref, *outs):
    strip_out, h_ref, l_ref = outs
    half = own_ref.shape[0] - 8
    step = step_of([own_ref[half:, :128], other_ref[half:, :128]], count)
    strip = strip_ref[...] - step * grad_ref[...]
    strip_out[...] = strip
    h_ref[...], l_ref[...] = split(strip)


def step_kernel(count, held_ref, grad_ref, *refs):
    step = step_of([t[...] for t in refs[:-1]], count)
    refs[-1][...] = held_ref[...] - step * grad_ref[...]


def last_gradient_kernel(share, *refs):
    parts, (grad_ref, tile_ref), sum_ref = refs[:-3], refs[-3:-1], refs[-1]
    half = sum_ref.shape[0]
    total = parts[0][:half, :]
    for ref in parts[1:]:
        total = total + ref[...]
    sum_ref[...] = total
    tile_ref[...] = tile_squares(total)
    chip, _ = place()
    grad_ref[...] = sum_ref[aligned(chip, share), :]


def last_step_kernel(count, message_ref, grad_ref, own_ref, other_ref, out_ref):
    step = step_of([own_ref[...], other_ref[...]], count)
    held = message_ref[message_ref.shape[0] - grad_ref.shape[0] :, :]
    out_ref[...] = held - step * grad_ref[...]


def on_device(readings, coverage, pixel_factors, date_factors):
    pixels, rank = pixel_factors.shape
    share = date_factors.shape[0]
    n = lax.axis_size("sub")
    blocks = lax.axis_size("blk")
    nx = n // CORES
    dates = share * n
    half = share * nx
    pixel_count = pixels * n * rank
    date_count = dates * rank
    work = pixels * dates * rank

    def moved(a, dx, dc):
        return (a // CORES + dx) % nx * CORES + (a % CORES + dc) % CORES

    def within(value, dx, dc):
        pairs = [(a, moved(a, dx, dc)) for a in range(n)]
        return lax.ppermute(value, "sub", pairs)

    def onward(value, dx):
        pairs = [
            (b * n + a, (b + 1) % blocks * n + moved(a, dx, 0))
            for b in range(blocks) for a in range(n)
        ]
        return lax.ppermute(value, ("blk", "sub"), pairs)

    def chips(value):
        return [value] + [within(value, dx, 0) for dx in range(1, nx)]

    strip_shapes = [shape(pixels, rank)] + [shape(pixels, rank, BF16)] * 2
    part_shapes = [shape(half, rank)] + [shape(half, pixels, BF16)] * 2
    part_shapes += [shape(half, rank)]

    def prepared(stratum, grant, *args):
        kinds = [F32, jnp.int32, F32][: len(args)]
        outs = [shape(dates, pixels)]
        if len(args) == 3:
            outs += strip_shapes
        scratch = [pltpu.VMEM((pixels, args[0].shape[2]), kind) for kind in kinds]
        scratch.append(pltpu.SemaphoreType.DMA((len(chunks_of(pixels)), len(args))))
        return call(
            functools.partial(prepare_kernel, stratum, share), outs, *args,
            where=HBM, scratch=scratch, grant=grant,
        )

    others = [within(date_factors, dx, 1) for dx in range(nx)]
    owns = chips(date_factors)
    old = onward(date_factors, 0)
    values, strip, *halves = prepared(0, WIDE, readings, coverage, pixel_factors)
    values_1, = prepared(1, GRANT, readings, coverage)
    send, h0, l0, b0 = call(
        functools.partial(first_send_kernel, nx), part_shapes,
        *others, values, *halves, flops=6 * work,
    )
    got = within(send, 0, 1)
    keep, h1, l1, b1 = call(
        functools.partial(first_keep_kernel, nx), part_shapes,
        *owns, values, *halves, flops=6 * work,
    )
    mine = keep + got
    came = [onward(mine, dx) for dx in range(nx)]
    grad, tile = call(
        gradient_kernel, [shape(pixels, rank), shape(8, rank)],
        strip, h0, l0, h1, l1, b0, b1, flops=6 * work,
    )
    messages = chips(jnp.concatenate([old, tile], 0))
    own_message, = call(join_kernel, [shape(half + 8, rank)], *messages)
    other_message = within(own_message, 0, 1)
    strip, *halves = call(
        functools.partial(first_step_kernel, pixel_count), strip_shapes,
        own_message, other_message, strip, grad,
    )
    own_grad = sum(came[1:], came[0])
    other_grad = within(own_grad, 0, 1)

    send, h0, l0, b0 = call(
        functools.partial(later_send_kernel, date_count), part_shapes,
        own_grad, other_grad, other_message, values_1, *halves, flops=6 * work,
    )
    got = within(send, 0, 1)
    keep, h1, l1, b1, own = call(
        functools.partial(later_keep_kernel, date_count, share),
        part_shapes + [shape(share, rank)],
        own_grad, other_grad, own_message, values_1, *halves, flops=6 * work,
    )
    mine = keep + got
    came = [onward(jnp.concatenate([mine, own], 0), 0)]
    came += [onward(mine, dx) for dx in range(1, nx)]
    grad, tile = call(
        gradient_kernel, [shape(pixels, rank), shape(8, 128)],
        strip, h0, l0, h1, l1, b0, b1, flops=6 * work,
    )
    tiles = chips(tile)
    tile = sum(tiles[1:], tiles[0])
    other_tile = within(tile, 0, 1)
    strip, = call(
        functools.partial(step_kernel, pixel_count), [shape(pixels, rank)],
        strip, grad, tile, other_tile,
    )
    date_grad, tile = call(
        functools.partial(last_gradient_kernel, share),
        [shape(share, rank), shape(8, 128)], *came,
        scratch=[pltpu.VMEM((half, rank), F32)],
    )
    other_tile = within(tile, 0, 1)
    date_out, = call(
        functools.partial(last_step_kernel, date_count), [shape(share, rank)],
        came[0], date_grad, tile, other_tile,
    )
    return strip, date_out


def solution(mesh):
    spec = P(("parts", "blk", "sub"), None)
    stacked = P(None, ("parts", "blk", "sub"), None)

    return jax.shard_map(
        on_device, mesh=mesh, in_specs=(stacked, stacked, spec, spec),
        out_specs=(spec, spec), check_vma=False,
    )
```

```python
import functools

import jax
import jax.numpy as jnp
from jax import lax
from jax.experimental import pallas as pl
from jax.experimental.pallas import tpu as pltpu
from jax.sharding import PartitionSpec as P


step_size = 0.05
ridge = 0.1
epsilon = 1e-06

CORES = 2
CHUNK = 256
HIDDEN = 1e9
GRANT = 16 << 20
WIDE = 53_000_000
F32 = jnp.float32
BF16 = jnp.bfloat16

VMEM = pl.BlockSpec(memory_space=pltpu.VMEM)
HBM = pl.BlockSpec(memory_space=pltpu.HBM)

NN = (((1,), (0,)), ((), ()))
TN = (((0,), (0,)), ((), ()))


def split(value):
    high = value.astype(BF16)
    low = (value - high.astype(F32)).astype(BF16)
    return high, low


def product(a, b, dims):
    dot = functools.partial(
        lax.dot_general, dimension_numbers=dims, preferred_element_type=F32
    )
    (a_high, a_low), (b_high, b_low) = a, b
    return dot(a_high, b_high) + (dot(a_high, b_low) + dot(a_low, b_high))


def tile_squares(value):
    squares = value * value
    rows, columns = squares.shape
    folded = squares.reshape(rows // 8, 8, columns).sum(0)
    total = folded[:, :128]
    for start in range(128, columns, 128):
        total = total + folded[:, start : start + 128]
    return total


def step_of(tiles, count):
    total = tiles[0]
    for tile in tiles[1:]:
        total = total + tile
    mean = jnp.sum(total, axis=(0, 1), keepdims=True) / count
    return step_size / jnp.sqrt(mean + epsilon)


def call(kernel, outs, *args, where=VMEM, scratch=(), flops=0, grant=GRANT):
    size = sum(a.size * a.dtype.itemsize for a in list(args) + list(outs))
    return pl.pallas_call(
        kernel,
        out_shape=outs,
        in_specs=[where] * len(args),
        out_specs=[VMEM] * len(outs),
        scratch_shapes=list(scratch),
        compiler_params=pltpu.CompilerParams(vmem_limit_bytes=grant),
        cost_estimate=pl.CostEstimate(
            flops=flops, bytes_accessed=size, transcendentals=0
        ),
    )(*args)


def shape(rows, columns, dtype=F32):
    return jax.ShapeDtypeStruct((rows, columns), dtype)


def chunks_of(pixels):
    size = CHUNK if pixels % CHUNK == 0 else pixels
    return [pl.ds(start, size) for start in range(0, pixels, size)]


def place():
    at = lax.axis_index("sub")
    return at // CORES, lax.rem(at, CORES)


def aligned(index, size):
    return pl.ds(pl.multiple_of(index * size, size), size)


def prepare_kernel(stratum, share, *refs):
    with_strip = stratum == 0
    sources = refs[: 2 + with_strip]
    outs = refs[len(sources) : len(sources) + 1 + 5 * with_strip]
    buffers, sem = refs[len(sources) + len(outs) : -1], refs[-1]
    pixels, dates = buffers[0].shape
    nx = dates // share // CORES
    chunks = chunks_of(pixels)
    copies = []
    for at, chunk in enumerate(chunks):
        row = []
        for which, (source, buffer) in enumerate(zip(sources, buffers)):
            view = source.at[chunk] if which == 2 else source.at[stratum, chunk]
            copy = pltpu.make_async_copy(view, buffer.at[chunk], sem.at[at, which])
            copy.start()
            row.append(copy)
        copies.append(row)
    _, core = place()
    for chunk, row in zip(chunks, copies):
        for copy in row:
            copy.wait()
        seen = jnp.where(buffers[1][chunk, :] != 0, buffers[0][chunk, :], HIDDEN)
        turned = seen.T
        for at in range(nx * CORES):
            own = jnp.where(core == at % CORES, nx, 0)
            rows = aligned(own + at // CORES, share)
            outs[0][rows, chunk] = turned[at * share : (at + 1) * share]
        if with_strip:
            strip = buffers[2][chunk, :]
            outs[1][chunk, :] = strip
            outs[2][chunk, :], outs[3][chunk, :] = split(strip)
            outs[4][:, chunk], outs[5][:, chunk] = split(strip.T)


def errors_and_part(side, problem, block, high_ref, low_ref):
    values_ref, h_ref, l_ref, th_ref, tl_ref = problem
    half = block.shape[0]
    rows = slice(side * half, (side + 1) * half)
    block = split(block)
    total = None
    for chunk in chunks_of(values_ref.shape[1]):
        strip = (h_ref[chunk, :], l_ref[chunk, :])
        values = values_ref[rows, chunk]
        predicted = product(block, (th_ref[:, chunk], tl_ref[:, chunk]), NN)
        errors = jnp.where(values < HIDDEN, values - predicted, 0.0)
        errors = split(errors)
        high_ref[:, chunk], low_ref[:, chunk] = errors
        part = product(errors, strip, NN)
        total = part if total is None else total + part
    return -total


def with_ridge(part, block):
    chip, _ = place()
    return part + jnp.where(chip == 0, ridge, 0.0) * block


def assemble(shares, block_ref):
    nx = len(shares)
    share = shares[0].shape[0]
    chip, _ = place()
    for dx, ref in enumerate(shares):
        block_ref[aligned(lax.rem(chip - dx + nx, nx), share), :] = ref[...]


def first_send_kernel(nx, *refs):
    problem, outs = refs[2 * nx : 2 * nx + 5], refs[2 * nx + 5 :]
    send_ref, high_ref, low_ref, other_ref, own_ref = outs
    assemble(refs[nx : 2 * nx], own_ref)
    assemble(refs[:nx], other_ref)
    send_ref[...] = errors_and_part(0, problem, other_ref[...], high_ref, low_ref)


def first_keep_kernel(block_ref, *refs):
    problem, (keep_ref, high_ref, low_ref) = refs[:5], refs[5:]
    block = block_ref[...]
    part = errors_and_part(1, problem, block, high_ref, low_ref)
    keep_ref[...] = with_ridge(part, block)


def later_step(count, own_ref, other_ref):
    return step_of([tile_squares(own_ref[...]), tile_squares(other_ref[...])], count)


def later_send_kernel(count, own_ref, other_ref, old_ref, *refs):
    problem, (send_ref, high_ref, low_ref, block_ref) = refs[:5], refs[5:]
    step = later_step(count, own_ref, other_ref)
    block = old_ref[...] - step * other_ref[...]
    block_ref[...] = block
    send_ref[...] = errors_and_part(0, problem, block, high_ref, low_ref)


def later_keep_kernel(count, share, own_ref, other_ref, old_ref, *refs):
    problem, (keep_ref, high_ref, low_ref, block_ref, share_ref) = refs[:5], refs[5:]
    step = later_step(count, own_ref, other_ref)
    block = old_ref[...] - step * own_ref[...]
    block_ref[...] = block
    chip, _ = place()
    share_ref[...] = block_ref[aligned(chip, share), :]
    part = errors_and_part(1, problem, block, high_ref, low_ref)
    keep_ref[...] = with_ridge(part, block)


def pixel_gradient(strip_ref, errors, blocks):
    joined = [jnp.concatenate([ref[...] for ref in part], 0) for part in errors]
    block = jnp.concatenate([ref[...] for ref in blocks], 0)
    return ridge * strip_ref[...] - product(joined, split(block), TN)


def gradient_kernel(strip_ref, h0, l0, h1, l1, b0, b1, grad_ref, tile_ref):
    grad = pixel_gradient(strip_ref, ((h0, h1), (l0, l1)), (b0, b1))
    grad_ref[...] = grad
    tile_ref[...] = tile_squares(grad)


def first_step_kernel(count, strip_ref, grad_ref, own_ref, other_ref, *outs):
    strip_out, h_ref, l_ref, th_ref, tl_ref = outs
    step = step_of([own_ref[...], other_ref[...]], count)
    strip = strip_ref[...] - step * grad_ref[...]
    strip_out[...] = strip
    h_ref[...], l_ref[...] = split(strip)
    th_ref[...], tl_ref[...] = split(strip.T)


def step_kernel(count, held_ref, grad_ref, *refs):
    step = step_of([t[...] for t in refs[:-1]], count)
    refs[-1][...] = held_ref[...] - step * grad_ref[...]


def last_gradient_kernel(share, *refs):
    parts, (grad_ref, tile_ref), sum_ref = refs[:-3], refs[-3:-1], refs[-1]
    half = sum_ref.shape[0]
    total = parts[0][:half, :]
    for ref in parts[1:]:
        total = total + ref[...]
    sum_ref[...] = total
    tile_ref[...] = tile_squares(total)
    chip, _ = place()
    grad_ref[...] = sum_ref[aligned(chip, share), :]


def last_step_kernel(count, message_ref, grad_ref, own_ref, other_ref, out_ref):
    step = step_of([own_ref[...], other_ref[...]], count)
    held = message_ref[message_ref.shape[0] - grad_ref.shape[0] :, :]
    out_ref[...] = held - step * grad_ref[...]


def on_device(readings, coverage, pixel_factors, date_factors):
    pixels, rank = pixel_factors.shape
    share = date_factors.shape[0]
    n = lax.axis_size("sub")
    blocks = lax.axis_size("blk")
    nx = n // CORES
    dates = share * n
    half = share * nx
    pixel_count = pixels * n * rank
    date_count = dates * rank
    work = pixels * dates * rank

    def moved(a, dx, dc):
        return (a // CORES + dx) % nx * CORES + (a % CORES + dc) % CORES

    def within(value, dx, dc):
        pairs = [(a, moved(a, dx, dc)) for a in range(n)]
        return lax.ppermute(value, "sub", pairs)

    def onward(value, dx):
        pairs = [
            (b * n + a, (b + 1) % blocks * n + moved(a, dx, 0))
            for b in range(blocks) for a in range(n)
        ]
        return lax.ppermute(value, ("blk", "sub"), pairs)

    def chips(value):
        return [value] + [within(value, dx, 0) for dx in range(1, nx)]

    strip_shapes = [shape(pixels, rank)] + [shape(pixels, rank, BF16)] * 2
    strip_shapes += [shape(rank, pixels, BF16)] * 2
    part_shapes = [shape(half, rank)] + [shape(half, pixels, BF16)] * 2

    def prepared(stratum, grant, *args):
        kinds = [F32, jnp.int32, F32][: len(args)]
        outs = [shape(dates, pixels)]
        if len(args) == 3:
            outs += strip_shapes
        scratch = [pltpu.VMEM((pixels, args[0].shape[2]), kind) for kind in kinds]
        scratch.append(pltpu.SemaphoreType.DMA((len(chunks_of(pixels)), len(args))))
        return call(
            functools.partial(prepare_kernel, stratum, share), outs, *args,
            where=HBM, scratch=scratch, grant=grant,
        )

    others = [within(date_factors, dx, 1) for dx in range(nx)]
    owns = chips(date_factors)
    values, strip, *halves = prepared(0, WIDE, readings, coverage, pixel_factors)
    values_1, = prepared(1, GRANT, readings, coverage)
    send, h0, l0, b0, b1 = call(
        functools.partial(first_send_kernel, nx),
        part_shapes + [shape(half, rank)] * 2,
        *others, *owns, values, *halves, flops=6 * work,
    )
    got = within(send, 0, 1)
    old_half = onward(b1, 0)
    keep, h1, l1 = call(
        first_keep_kernel, part_shapes, b1, values, *halves, flops=6 * work
    )
    mine = keep + got
    came = [onward(mine, dx) for dx in range(nx)]
    grad, tile = call(
        gradient_kernel, [shape(pixels, rank), shape(8, 128)],
        strip, h0, l0, h1, l1, b0, b1, flops=6 * work,
    )
    tiles = chips(tile)
    tile = sum(tiles[1:], tiles[0])
    other_tile = within(tile, 0, 1)
    old_other = within(old_half, 0, 1)
    strip, *halves = call(
        functools.partial(first_step_kernel, pixel_count), strip_shapes,
        strip, grad, tile, other_tile,
    )
    own_grad = sum(came[1:], came[0])
    other_grad = within(own_grad, 0, 1)

    send, h0, l0, b0 = call(
        functools.partial(later_send_kernel, date_count),
        part_shapes + [shape(half, rank)],
        own_grad, other_grad, old_other, values_1, *halves, flops=6 * work,
    )
    got = within(send, 0, 1)
    keep, h1, l1, b1, own = call(
        functools.partial(later_keep_kernel, date_count, share),
        part_shapes + [shape(half, rank), shape(share, rank)],
        own_grad, other_grad, old_half, values_1, *halves, flops=6 * work,
    )
    mine = keep + got
    came = [onward(jnp.concatenate([mine, own], 0), 0)]
    came += [onward(mine, dx) for dx in range(1, nx)]
    grad, tile = call(
        gradient_kernel, [shape(pixels, rank), shape(8, 128)],
        strip, h0, l0, h1, l1, b0, b1, flops=6 * work,
    )
    tiles = chips(tile)
    tile = sum(tiles[1:], tiles[0])
    other_tile = within(tile, 0, 1)
    strip, = call(
        functools.partial(step_kernel, pixel_count), [shape(pixels, rank)],
        strip, grad, tile, other_tile,
    )
    date_grad, tile = call(
        functools.partial(last_gradient_kernel, share),
        [shape(share, rank), shape(8, 128)], *came,
        scratch=[pltpu.VMEM((half, rank), F32)],
    )
    other_tile = within(tile, 0, 1)
    date_out, = call(
        functools.partial(last_step_kernel, date_count), [shape(share, rank)],
        came[0], date_grad, tile, other_tile,
    )
    return strip, date_out


def solution(mesh):
    spec = P(("parts", "blk", "sub"), None)
    stacked = P(None, ("parts", "blk", "sub"), None)

    return jax.shard_map(
        on_device, mesh=mesh, in_specs=(stacked, stacked, spec, spec),
        out_specs=(spec, spec), check_vma=False,
    )
```

```python
import functools

import jax
import jax.numpy as jnp
from jax import lax
from jax.experimental import pallas as pl
from jax.experimental.pallas import tpu as pltpu
from jax.sharding import PartitionSpec as P


step_size = 0.05
ridge = 0.1
epsilon = 1e-06

CORES = 2
CHUNK = 256
HIDDEN = 1e9
GRANT = 16 << 20
WIDE = 53_000_000
F32 = jnp.float32
BF16 = jnp.bfloat16

VMEM = pl.BlockSpec(memory_space=pltpu.VMEM)
HBM = pl.BlockSpec(memory_space=pltpu.HBM)

NN = (((1,), (0,)), ((), ()))
TN = (((0,), (0,)), ((), ()))


def split(value):
    high = value.astype(BF16)
    low = (value - high.astype(F32)).astype(BF16)
    return high, low


def product(a, b, dims):
    dot = functools.partial(
        lax.dot_general, dimension_numbers=dims, preferred_element_type=F32
    )
    (a_high, a_low), (b_high, b_low) = a, b
    return dot(a_high, b_high) + (dot(a_high, b_low) + dot(a_low, b_high))


def tile_squares(value):
    squares = value * value
    rows, columns = squares.shape
    folded = squares.reshape(rows // 8, 8, columns).sum(0)
    total = folded[:, :128]
    for start in range(128, columns, 128):
        total = total + folded[:, start : start + 128]
    return total


def step_of(tiles, count):
    total = tiles[0]
    for tile in tiles[1:]:
        total = total + tile
    mean = jnp.sum(total, axis=(0, 1), keepdims=True) / count
    return step_size / jnp.sqrt(mean + epsilon)


def call(kernel, outs, *args, where=VMEM, scratch=(), flops=0, grant=GRANT):
    size = sum(a.size * a.dtype.itemsize for a in list(args) + list(outs))
    return pl.pallas_call(
        kernel,
        out_shape=outs,
        in_specs=[where] * len(args),
        out_specs=[VMEM] * len(outs),
        scratch_shapes=list(scratch),
        compiler_params=pltpu.CompilerParams(vmem_limit_bytes=grant),
        cost_estimate=pl.CostEstimate(
            flops=flops, bytes_accessed=size, transcendentals=0
        ),
    )(*args)


def shape(rows, columns, dtype=F32):
    return jax.ShapeDtypeStruct((rows, columns), dtype)


def chunks_of(pixels):
    size = CHUNK if pixels % CHUNK == 0 else pixels
    return [pl.ds(start, size) for start in range(0, pixels, size)]


def place():
    at = lax.axis_index("sub")
    return at // CORES, lax.rem(at, CORES)


def aligned(index, size):
    return pl.ds(pl.multiple_of(index * size, size), size)


def prepare_kernel(stratum, share, *refs):
    with_strip = stratum == 0
    sources = refs[: 2 + with_strip]
    outs = refs[len(sources) : len(sources) + 1 + 5 * with_strip]
    buffers, sem = refs[len(sources) + len(outs) : -1], refs[-1]
    pixels, dates = buffers[0].shape
    nx = dates // share // CORES
    chunks = chunks_of(pixels)
    copies = []
    for at, chunk in enumerate(chunks):
        row = []
        for which, (source, buffer) in enumerate(zip(sources, buffers)):
            view = source.at[chunk] if which == 2 else source.at[stratum, chunk]
            copy = pltpu.make_async_copy(view, buffer.at[chunk], sem.at[at, which])
            copy.start()
            row.append(copy)
        copies.append(row)
    _, core = place()
    for chunk, row in zip(chunks, copies):
        for copy in row:
            copy.wait()
        seen = jnp.where(buffers[1][chunk, :] != 0, buffers[0][chunk, :], HIDDEN)
        turned = seen.T
        for at in range(nx * CORES):
            own = jnp.where(core == at % CORES, nx, 0)
            rows = aligned(own + at // CORES, share)
            outs[0][rows, chunk] = turned[at * share : (at + 1) * share]
        if with_strip:
            strip = buffers[2][chunk, :]
            outs[1][chunk, :] = strip
            outs[2][chunk, :], outs[3][chunk, :] = split(strip)
            outs[4][:, chunk], outs[5][:, chunk] = split(strip.T)


def errors_and_part(side, problem, block, high_ref, low_ref):
    values_ref, h_ref, l_ref, th_ref, tl_ref = problem
    half = block.shape[0]
    rows = slice(side * half, (side + 1) * half)
    block = split(block)
    total = None
    for chunk in chunks_of(values_ref.shape[1]):
        strip = (h_ref[chunk, :], l_ref[chunk, :])
        values = values_ref[rows, chunk]
        predicted = product(block, (th_ref[:, chunk], tl_ref[:, chunk]), NN)
        errors = jnp.where(values < HIDDEN, values - predicted, 0.0)
        errors = split(errors)
        high_ref[:, chunk], low_ref[:, chunk] = errors
        part = product(errors, strip, NN)
        total = part if total is None else total + part
    return -total


def with_ridge(part, block):
    chip, _ = place()
    return part + jnp.where(chip == 0, ridge, 0.0) * block


def assemble(shares, block_ref):
    nx = len(shares)
    share = shares[0].shape[0]
    chip, _ = place()
    for dx, ref in enumerate(shares):
        block_ref[aligned(lax.rem(chip - dx + nx, nx), share), :] = ref[...]


def first_send_kernel(nx, *refs):
    problem, (send_ref, high_ref, low_ref, block_ref) = refs[nx : nx + 5], refs[nx + 5 :]
    assemble(refs[:nx], block_ref)
    send_ref[...] = errors_and_part(0, problem, block_ref[...], high_ref, low_ref)


def first_keep_kernel(nx, *refs):
    problem, (keep_ref, high_ref, low_ref, block_ref) = refs[nx : nx + 5], refs[nx + 5 :]
    assemble(refs[:nx], block_ref)
    block = block_ref[...]
    part = errors_and_part(1, problem, block, high_ref, low_ref)
    keep_ref[...] = with_ridge(part, block)


def join_kernel(*refs):
    assemble(refs[:-1], refs[-1])


def later_step(count, own_ref, other_ref):
    return step_of([tile_squares(own_ref[...]), tile_squares(other_ref[...])], count)


def later_send_kernel(count, own_ref, other_ref, old_ref, *refs):
    problem, (send_ref, high_ref, low_ref, block_ref) = refs[:5], refs[5:]
    step = later_step(count, own_ref, other_ref)
    block = old_ref[...] - step * other_ref[...]
    block_ref[...] = block
    send_ref[...] = errors_and_part(0, problem, block, high_ref, low_ref)


def later_keep_kernel(count, share, own_ref, other_ref, old_ref, *refs):
    problem, (keep_ref, high_ref, low_ref, block_ref, share_ref) = refs[:5], refs[5:]
    step = later_step(count, own_ref, other_ref)
    block = old_ref[...] - step * own_ref[...]
    block_ref[...] = block
    chip, _ = place()
    share_ref[...] = block_ref[aligned(chip, share), :]
    part = errors_and_part(1, problem, block, high_ref, low_ref)
    keep_ref[...] = with_ridge(part, block)


def pixel_gradient(strip_ref, errors, blocks):
    joined = [jnp.concatenate([ref[...] for ref in part], 0) for part in errors]
    block = jnp.concatenate([ref[...] for ref in blocks], 0)
    return ridge * strip_ref[...] - product(joined, split(block), TN)


def gradient_kernel(strip_ref, h0, l0, h1, l1, b0, b1, grad_ref, tile_ref):
    grad = pixel_gradient(strip_ref, ((h0, h1), (l0, l1)), (b0, b1))
    grad_ref[...] = grad
    tile_ref[...] = tile_squares(grad)


def first_step_kernel(count, strip_ref, grad_ref, own_ref, other_ref, *outs):
    strip_out, h_ref, l_ref, th_ref, tl_ref = outs
    step = step_of([own_ref[...], other_ref[...]], count)
    strip = strip_ref[...] - step * grad_ref[...]
    strip_out[...] = strip
    h_ref[...], l_ref[...] = split(strip)
    th_ref[...], tl_ref[...] = split(strip.T)


def step_kernel(count, held_ref, grad_ref, *refs):
    step = step_of([t[...] for t in refs[:-1]], count)
    refs[-1][...] = held_ref[...] - step * grad_ref[...]


def last_gradient_kernel(share, *refs):
    parts, (grad_ref, tile_ref), sum_ref = refs[:-3], refs[-3:-1], refs[-1]
    total = parts[0][...]
    for ref in parts[1:]:
        total = total + ref[...]
    sum_ref[...] = total
    tile_ref[...] = tile_squares(total)
    chip, _ = place()
    grad_ref[...] = sum_ref[aligned(chip, share), :]


def on_device(readings, coverage, pixel_factors, date_factors):
    pixels, rank = pixel_factors.shape
    share = date_factors.shape[0]
    n = lax.axis_size("sub")
    blocks = lax.axis_size("blk")
    nx = n // CORES
    dates = share * n
    half = share * nx
    pixel_count = pixels * n * rank
    date_count = dates * rank
    work = pixels * dates * rank

    def moved(a, dx, dc):
        return (a // CORES + dx) % nx * CORES + (a % CORES + dc) % CORES

    def within(value, dx, dc):
        pairs = [(a, moved(a, dx, dc)) for a in range(n)]
        return lax.ppermute(value, "sub", pairs)

    def onward(value, dx):
        pairs = [
            (b * n + a, (b + 1) % blocks * n + moved(a, dx, 0))
            for b in range(blocks) for a in range(n)
        ]
        return lax.ppermute(value, ("blk", "sub"), pairs)

    def chips(value):
        return [value] + [within(value, dx, 0) for dx in range(1, nx)]

    strip_shapes = [shape(pixels, rank)] + [shape(pixels, rank, BF16)] * 2
    strip_shapes += [shape(rank, pixels, BF16)] * 2
    part_shapes = [shape(half, rank)] + [shape(half, pixels, BF16)] * 2

    def prepared(stratum, grant, *args):
        kinds = [F32, jnp.int32, F32][: len(args)]
        outs = [shape(dates, pixels)]
        if len(args) == 3:
            outs += strip_shapes
        scratch = [pltpu.VMEM((pixels, args[0].shape[2]), kind) for kind in kinds]
        scratch.append(pltpu.SemaphoreType.DMA((len(chunks_of(pixels)), len(args))))
        return call(
            functools.partial(prepare_kernel, stratum, share), outs, *args,
            where=HBM, scratch=scratch, grant=grant,
        )

    others = [within(date_factors, dx, 1) for dx in range(nx)]
    owns = chips(date_factors)
    old = onward(date_factors, 0)
    values, strip, *halves = prepared(0, WIDE, readings, coverage, pixel_factors)
    values_1, = prepared(1, GRANT, readings, coverage)
    send, h0, l0, b0 = call(
        functools.partial(first_send_kernel, nx), part_shapes + [shape(half, rank)],
        *others, values, *halves, flops=6 * work,
    )
    got = within(send, 0, 1)
    keep, h1, l1, b1 = call(
        functools.partial(first_keep_kernel, nx), part_shapes + [shape(half, rank)],
        *owns, values, *halves, flops=6 * work,
    )
    mine = keep + got
    came = [onward(mine, dx) for dx in range(nx)]
    grad, tile = call(
        gradient_kernel, [shape(pixels, rank), shape(8, 128)],
        strip, h0, l0, h1, l1, b0, b1, flops=6 * work,
    )
    tiles = chips(tile)
    tile = sum(tiles[1:], tiles[0])
    other_tile = within(tile, 0, 1)
    olds = chips(old)
    old_half, = call(join_kernel, [shape(half, rank)], *olds)
    old_other = within(old_half, 0, 1)
    strip, *halves = call(
        functools.partial(first_step_kernel, pixel_count), strip_shapes,
        strip, grad, tile, other_tile,
    )
    own_grad = sum(came[1:], came[0])
    other_grad = within(own_grad, 0, 1)

    send, h0, l0, b0 = call(
        functools.partial(later_send_kernel, date_count),
        part_shapes + [shape(half, rank)],
        own_grad, other_grad, old_other, values_1, *halves, flops=6 * work,
    )
    got = within(send, 0, 1)
    keep, h1, l1, b1, own = call(
        functools.partial(later_keep_kernel, date_count, share),
        part_shapes + [shape(half, rank), shape(share, rank)],
        own_grad, other_grad, old_half, values_1, *halves, flops=6 * work,
    )
    mine = keep + got
    came = [onward(mine, dx) for dx in range(nx)]
    held = onward(own, 0)
    grad, tile = call(
        gradient_kernel, [shape(pixels, rank), shape(8, 128)],
        strip, h0, l0, h1, l1, b0, b1, flops=6 * work,
    )
    tiles = chips(tile)
    tile = sum(tiles[1:], tiles[0])
    other_tile = within(tile, 0, 1)
    strip, = call(
        functools.partial(step_kernel, pixel_count), [shape(pixels, rank)],
        strip, grad, tile, other_tile,
    )
    date_grad, tile = call(
        functools.partial(last_gradient_kernel, share),
        [shape(share, rank), shape(8, 128)], *came,
        scratch=[pltpu.VMEM((half, rank), F32)],
    )
    other_tile = within(tile, 0, 1)
    date_out, = call(
        functools.partial(step_kernel, date_count), [shape(share, rank)],
        held, date_grad, tile, other_tile,
    )
    return strip, date_out


def solution(mesh):
    spec = P(("parts", "blk", "sub"), None)
    stacked = P(None, ("parts", "blk", "sub"), None)

    return jax.shard_map(
        on_device, mesh=mesh, in_specs=(stacked, stacked, spec, spec),
        out_specs=(spec, spec), check_vma=False,
    )
```

```python
import functools

import jax
import jax.numpy as jnp
from jax import lax
from jax.experimental import pallas as pl
from jax.experimental.pallas import tpu as pltpu
from jax.sharding import PartitionSpec as P


step_size = 0.05
ridge = 0.1
epsilon = 1e-06

CORES = 2
CHUNK = 256
HIDDEN = 1e9
GRANT = 16 << 20
WIDE = 53_000_000
F32 = jnp.float32
BF16 = jnp.bfloat16

VMEM = pl.BlockSpec(memory_space=pltpu.VMEM)
HBM = pl.BlockSpec(memory_space=pltpu.HBM)

NN = (((1,), (0,)), ((), ()))
TN = (((0,), (0,)), ((), ()))


def split(value):
    high = value.astype(BF16)
    low = (value - high.astype(F32)).astype(BF16)
    return high, low


def product(a, b, dims):
    dot = functools.partial(
        lax.dot_general, dimension_numbers=dims, preferred_element_type=F32
    )
    (a_high, a_low), (b_high, b_low) = a, b
    if dims == NN:
        rows = a_high.shape[0]
        both = dot(jnp.concatenate([a_high, a_low], 0), b_high)
        return both[:rows] + (dot(a_high, b_low) + both[rows:])
    return dot(a_high, b_high) + (dot(a_high, b_low) + dot(a_low, b_high))


def tile_squares(value):
    squares = value * value
    rows, columns = squares.shape
    folded = squares.reshape(rows // 8, 8, columns).sum(0)
    total = folded[:, :128]
    for start in range(128, columns, 128):
        total = total + folded[:, start : start + 128]
    return total


def step_of(tiles, count):
    total = tiles[0]
    for tile in tiles[1:]:
        total = total + tile
    mean = jnp.sum(total, axis=(0, 1), keepdims=True) / count
    return step_size / jnp.sqrt(mean + epsilon)


def call(kernel, outs, *args, where=VMEM, scratch=(), flops=0, grant=GRANT):
    size = sum(a.size * a.dtype.itemsize for a in list(args) + list(outs))
    return pl.pallas_call(
        kernel,
        out_shape=outs,
        in_specs=[where] * len(args),
        out_specs=[VMEM] * len(outs),
        scratch_shapes=list(scratch),
        compiler_params=pltpu.CompilerParams(vmem_limit_bytes=grant),
        cost_estimate=pl.CostEstimate(
            flops=flops, bytes_accessed=size, transcendentals=0
        ),
    )(*args)


def shape(rows, columns, dtype=F32):
    return jax.ShapeDtypeStruct((rows, columns), dtype)


def chunks_of(pixels):
    size = CHUNK if pixels % CHUNK == 0 else pixels
    return [pl.ds(start, size) for start in range(0, pixels, size)]


def place():
    at = lax.axis_index("sub")
    return at // CORES, lax.rem(at, CORES)


def aligned(index, size):
    return pl.ds(pl.multiple_of(index * size, size), size)


def prepare_kernel(stratum, share, *refs):
    with_strip = stratum == 0
    sources = refs[: 2 + with_strip]
    outs = refs[len(sources) : len(sources) + 1 + 5 * with_strip]
    buffers, sem = refs[len(sources) + len(outs) : -1], refs[-1]
    pixels, dates = buffers[0].shape
    nx = dates // share // CORES
    chunks = chunks_of(pixels)
    copies = []
    for at, chunk in enumerate(chunks):
        row = []
        for which, (source, buffer) in enumerate(zip(sources, buffers)):
            view = source.at[chunk] if which == 2 else source.at[stratum, chunk]
            copy = pltpu.make_async_copy(view, buffer.at[chunk], sem.at[at, which])
            copy.start()
            row.append(copy)
        copies.append(row)
    _, core = place()
    for chunk, row in zip(chunks, copies):
        for copy in row:
            copy.wait()
        seen = jnp.where(buffers[1][chunk, :] != 0, buffers[0][chunk, :], HIDDEN)
        turned = seen.T
        for at in range(nx * CORES):
            own = jnp.where(core == (at + stratum) % CORES, nx, 0)
            rows = aligned(own + at // CORES, share)
            outs[0][rows, chunk] = turned[at * share : (at + 1) * share]
        if with_strip:
            strip = buffers[2][chunk, :]
            outs[1][chunk, :] = strip
            outs[2][chunk, :], outs[3][chunk, :] = split(strip)
            outs[4][:, chunk], outs[5][:, chunk] = split(strip.T)


def errors_and_part(side, problem, block, high_ref, low_ref):
    values_ref, h_ref, l_ref, th_ref, tl_ref = problem
    half = block.shape[0]
    rows = slice(side * half, (side + 1) * half)
    block = split(block)
    total = None
    for chunk in chunks_of(values_ref.shape[1]):
        strip = (h_ref[chunk, :], l_ref[chunk, :])
        values = values_ref[rows, chunk]
        predicted = product(block, (th_ref[:, chunk], tl_ref[:, chunk]), NN)
        errors = jnp.where(values < HIDDEN, values - predicted, 0.0)
        errors = split(errors)
        high_ref[:, chunk], low_ref[:, chunk] = errors
        part = product(errors, strip, NN)
        total = part if total is None else total + part
    return -total


def with_ridge(part, block):
    chip, _ = place()
    return part + jnp.where(chip == 0, ridge, 0.0) * block


def assemble(shares, block_ref):
    nx = len(shares)
    share = shares[0].shape[0]
    chip, _ = place()
    for dx, ref in enumerate(shares):
        block_ref[aligned(lax.rem(chip - dx + nx, nx), share), :] = ref[...]


def first_send_kernel(nx, *refs):
    problem, (send_ref, high_ref, low_ref, block_ref) = refs[nx : nx + 5], refs[nx + 5 :]
    assemble(refs[:nx], block_ref)
    send_ref[...] = errors_and_part(0, problem, block_ref[...], high_ref, low_ref)


def first_keep_kernel(nx, *refs):
    problem, (keep_ref, high_ref, low_ref, block_ref) = refs[nx : nx + 5], refs[nx + 5 :]
    assemble(refs[:nx], block_ref)
    block = block_ref[...]
    part = errors_and_part(1, problem, block, high_ref, low_ref)
    keep_ref[...] = with_ridge(part, block)


def join_kernel(*refs):
    assemble(refs[:-1], refs[-1])


def later_step(count, own_ref, other_ref):
    return step_of([tile_squares(own_ref[...]), tile_squares(other_ref[...])], count)


def later_send_kernel(count, own_ref, other_ref, old_ref, *refs):
    problem, (send_ref, high_ref, low_ref, block_ref) = refs[:5], refs[5:]
    step = later_step(count, own_ref, other_ref)
    block = old_ref[...] - step * other_ref[...]
    block_ref[...] = block
    send_ref[...] = errors_and_part(0, problem, block, high_ref, low_ref)


def later_keep_kernel(count, share, own_ref, other_ref, old_ref, *refs):
    problem, (keep_ref, high_ref, low_ref, block_ref, share_ref) = refs[:5], refs[5:]
    step = later_step(count, own_ref, other_ref)
    block = old_ref[...] - step * own_ref[...]
    block_ref[...] = block
    chip, _ = place()
    share_ref[...] = block_ref[aligned(chip, share), :]
    part = errors_and_part(1, problem, block, high_ref, low_ref)
    keep_ref[...] = with_ridge(part, block)


def pixel_gradient(strip_ref, errors, blocks):
    joined = [jnp.concatenate([ref[...] for ref in part], 0) for part in errors]
    block = jnp.concatenate([ref[...] for ref in blocks], 0)
    return ridge * strip_ref[...] - product(joined, split(block), TN)


def gradient_kernel(strip_ref, h0, l0, h1, l1, b0, b1, grad_ref, tile_ref):
    grad = pixel_gradient(strip_ref, ((h0, h1), (l0, l1)), (b0, b1))
    grad_ref[...] = grad
    tile_ref[...] = tile_squares(grad)


def first_step_kernel(count, strip_ref, grad_ref, own_ref, other_ref, *outs):
    strip_out, h_ref, l_ref, th_ref, tl_ref = outs
    step = step_of([own_ref[...], other_ref[...]], count)
    strip = strip_ref[...] - step * grad_ref[...]
    strip_out[...] = strip
    h_ref[...], l_ref[...] = split(strip)
    th_ref[...], tl_ref[...] = split(strip.T)


def step_kernel(count, held_ref, grad_ref, *refs):
    step = step_of([t[...] for t in refs[:-1]], count)
    refs[-1][...] = held_ref[...] - step * grad_ref[...]


def last_gradient_kernel(share, *refs):
    parts, (grad_ref, tile_ref), sum_ref = refs[:-3], refs[-3:-1], refs[-1]
    total = parts[0][...]
    for ref in parts[1:]:
        total = total + ref[...]
    sum_ref[...] = total
    tile_ref[...] = tile_squares(total)
    chip, _ = place()
    grad_ref[...] = sum_ref[aligned(chip, share), :]


def on_device(readings, coverage, pixel_factors, date_factors):
    pixels, rank = pixel_factors.shape
    share = date_factors.shape[0]
    n = lax.axis_size("sub")
    blocks = lax.axis_size("blk")
    nx = n // CORES
    dates = share * n
    half = share * nx
    pixel_count = pixels * n * rank
    date_count = dates * rank
    work = pixels * dates * rank

    def moved(a, dx, dc):
        return (a // CORES + dx) % nx * CORES + (a % CORES + dc) % CORES

    def within(value, dx, dc):
        pairs = [(a, moved(a, dx, dc)) for a in range(n)]
        return lax.ppermute(value, "sub", pairs)

    def onward(value, dx):
        pairs = [
            (b * n + a, (b + 1) % blocks * n + moved(a, dx, 1))
            for b in range(blocks) for a in range(n)
        ]
        return lax.ppermute(value, ("blk", "sub"), pairs)

    def chips(value):
        return [value] + [within(value, dx, 0) for dx in range(1, nx)]

    strip_shapes = [shape(pixels, rank)] + [shape(pixels, rank, BF16)] * 2
    strip_shapes += [shape(rank, pixels, BF16)] * 2
    part_shapes = [shape(half, rank)] + [shape(half, pixels, BF16)] * 2

    def prepared(stratum, grant, *args):
        kinds = [F32, jnp.int32, F32][: len(args)]
        outs = [shape(dates, pixels)]
        if len(args) == 3:
            outs += strip_shapes
        scratch = [
            pltpu.VMEM((pixels, a.shape[-1]), kind) for a, kind in zip(args, kinds)
        ]
        scratch.append(pltpu.SemaphoreType.DMA((len(chunks_of(pixels)), len(args))))
        return call(
            functools.partial(prepare_kernel, stratum, share), outs, *args,
            where=HBM, scratch=scratch, grant=grant,
        )

    others = [within(date_factors, dx, 1) for dx in range(nx)]
    owns = chips(date_factors)
    old = onward(date_factors, 0)
    values, strip, *halves = prepared(0, WIDE, readings, coverage, pixel_factors)
    values_1, = prepared(1, GRANT, readings, coverage)
    send, h0, l0, b0 = call(
        functools.partial(first_send_kernel, nx), part_shapes + [shape(half, rank)],
        *others, values, *halves, flops=6 * work,
    )
    got = within(send, 0, 1)
    keep, h1, l1, b1 = call(
        functools.partial(first_keep_kernel, nx), part_shapes + [shape(half, rank)],
        *owns, values, *halves, flops=6 * work,
    )
    mine = keep + got
    came = [onward(mine, dx) for dx in range(nx)]
    grad, tile = call(
        gradient_kernel, [shape(pixels, rank), shape(8, 128)],
        strip, h0, l0, h1, l1, b0, b1, flops=6 * work,
    )
    tiles = [tile] + [within(tile, dx, 1) for dx in range(1, nx)]
    tile = sum(tiles[1:], tiles[0])
    other_tile = within(tile, 0, 1)
    olds = chips(old)
    old_half, = call(join_kernel, [shape(half, rank)], *olds)
    old_other = within(old_half, 0, 1)
    strip, *halves = call(
        functools.partial(first_step_kernel, pixel_count), strip_shapes,
        strip, grad, tile, other_tile,
    )
    own_grad = sum(came[1:], came[0])
    other_grad = within(own_grad, 0, 1)

    send, h0, l0, b0 = call(
        functools.partial(later_send_kernel, date_count),
        part_shapes + [shape(half, rank)],
        own_grad, other_grad, old_other, values_1, *halves, flops=6 * work,
    )
    got = within(send, 0, 1)
    keep, h1, l1, b1, own = call(
        functools.partial(later_keep_kernel, date_count, share),
        part_shapes + [shape(half, rank), shape(share, rank)],
        own_grad, other_grad, old_half, values_1, *halves, flops=6 * work,
    )
    mine = keep + got
    came = [onward(mine, dx) for dx in range(nx)]
    held = onward(own, 0)
    grad, tile = call(
        gradient_kernel, [shape(pixels, rank), shape(8, 128)],
        strip, h0, l0, h1, l1, b0, b1, flops=6 * work,
    )
    tiles = [tile] + [within(tile, dx, 1) for dx in range(1, nx)]
    tile = sum(tiles[1:], tiles[0])
    other_tile = within(tile, 0, 1)
    strip, = call(
        functools.partial(step_kernel, pixel_count), [shape(pixels, rank)],
        strip, grad, tile, other_tile,
    )
    date_grad, tile = call(
        functools.partial(last_gradient_kernel, share),
        [shape(share, rank), shape(8, 128)], *came,
        scratch=[pltpu.VMEM((half, rank), F32)],
    )
    other_tile = within(tile, 0, 1)
    date_out, = call(
        functools.partial(step_kernel, date_count), [shape(share, rank)],
        held, date_grad, tile, other_tile,
    )
    return strip, date_out


def solution(mesh):
    spec = P(("parts", "blk", "sub"), None)
    stacked = P(None, ("parts", "blk", "sub"), None)

    return jax.shard_map(
        on_device, mesh=mesh, in_specs=(stacked, stacked, spec, spec),
        out_specs=(spec, spec), check_vma=False,
    )
```

```python
import functools

import jax
import jax.numpy as jnp
from jax import lax
from jax.experimental import pallas as pl
from jax.experimental.pallas import tpu as pltpu
from jax.sharding import PartitionSpec as P


step_size = 0.05
ridge = 0.1
epsilon = 1e-06

CORES = 2
CHUNK = 256
HIDDEN = 1e9
GRANT = 16 << 20
WIDE = 53_000_000
F32 = jnp.float32
BF16 = jnp.bfloat16

VMEM = pl.BlockSpec(memory_space=pltpu.VMEM)
HBM = pl.BlockSpec(memory_space=pltpu.HBM)

NN = (((1,), (0,)), ((), ()))
TN = (((0,), (0,)), ((), ()))


def split(value):
    high = value.astype(BF16)
    low = (value - high.astype(F32)).astype(BF16)
    return high, low


def product(a, b, dims):
    dot = functools.partial(
        lax.dot_general, dimension_numbers=dims, preferred_element_type=F32
    )
    (a_high, a_low), (b_high, b_low) = a, b
    return dot(a_high, b_high) + (dot(a_high, b_low) + dot(a_low, b_high))


def tile_squares(value):
    squares = value * value
    rows, columns = squares.shape
    folded = squares.reshape(rows // 8, 8, columns).sum(0)
    total = folded[:, :128]
    for start in range(128, columns, 128):
        total = total + folded[:, start : start + 128]
    return total


def step_of(tiles, count):
    total = tiles[0]
    for tile in tiles[1:]:
        total = total + tile
    mean = jnp.sum(total, axis=(0, 1), keepdims=True) / count
    return step_size / jnp.sqrt(mean + epsilon)


def call(kernel, outs, *args, where=VMEM, scratch=(), flops=0, grant=GRANT):
    size = sum(a.size * a.dtype.itemsize for a in list(args) + list(outs))
    return pl.pallas_call(
        kernel,
        out_shape=outs,
        in_specs=[where] * len(args),
        out_specs=[VMEM] * len(outs),
        scratch_shapes=list(scratch),
        compiler_params=pltpu.CompilerParams(vmem_limit_bytes=grant),
        cost_estimate=pl.CostEstimate(
            flops=flops, bytes_accessed=size, transcendentals=0
        ),
    )(*args)


def shape(rows, columns, dtype=F32):
    return jax.ShapeDtypeStruct((rows, columns), dtype)


def chunks_of(pixels):
    size = CHUNK if pixels % CHUNK == 0 else pixels
    return [pl.ds(start, size) for start in range(0, pixels, size)]


def place():
    at = lax.axis_index("sub")
    return at // CORES, lax.rem(at, CORES)


def aligned(index, size):
    return pl.ds(pl.multiple_of(index * size, size), size)


def prepare_kernel(stratum, share, *refs):
    with_strip = stratum == 0
    sources = refs[: 2 + with_strip]
    outs = refs[len(sources) : len(sources) + 1 + 5 * with_strip]
    buffers, sem = refs[len(sources) + len(outs) : -1], refs[-1]
    pixels, dates = buffers[0].shape
    nx = dates // share // CORES
    chunks = chunks_of(pixels)
    copies = []
    for at, chunk in enumerate(chunks):
        row = []
        for which, (source, buffer) in enumerate(zip(sources, buffers)):
            view = source.at[chunk] if which == 2 else source.at[stratum, chunk]
            copy = pltpu.make_async_copy(view, buffer.at[chunk], sem.at[at, which])
            copy.start()
            row.append(copy)
        copies.append(row)
    _, core = place()
    for chunk, row in zip(chunks, copies):
        for copy in row:
            copy.wait()
        seen = jnp.where(buffers[1][chunk, :] != 0, buffers[0][chunk, :], HIDDEN)
        turned = seen.T
        for at in range(nx * CORES):
            own = jnp.where(core == (at + stratum) % CORES, nx, 0)
            rows = aligned(own + at // CORES, share)
            outs[0][rows, chunk] = turned[at * share : (at + 1) * share]
        if with_strip:
            strip = buffers[2][chunk, :]
            outs[1][chunk, :] = strip
            outs[2][chunk, :], outs[3][chunk, :] = split(strip)
            outs[4][:, chunk], outs[5][:, chunk] = split(strip.T)


def errors_and_part(side, problem, block, high_ref, low_ref):
    values_ref, h_ref, l_ref, th_ref, tl_ref = problem
    half = block.shape[0]
    rows = slice(side * half, (side + 1) * half)
    block = split(block)
    total = None
    for chunk in chunks_of(values_ref.shape[1]):
        strip = (h_ref[chunk, :], l_ref[chunk, :])
        values = values_ref[rows, chunk]
        predicted = product(block, (th_ref[:, chunk], tl_ref[:, chunk]), NN)
        errors = jnp.where(values < HIDDEN, values - predicted, 0.0)
        errors = split(errors)
        high_ref[:, chunk], low_ref[:, chunk] = errors
        part = product(errors, strip, NN)
        total = part if total is None else total + part
    return -total


def with_ridge(part, block):
    chip, _ = place()
    return part + jnp.where(chip == 0, ridge, 0.0) * block


def assemble(shares, block_ref):
    nx = len(shares)
    share = shares[0].shape[0]
    chip, _ = place()
    for dx, ref in enumerate(shares):
        block_ref[aligned(lax.rem(chip - dx + nx, nx), share), :] = ref[...]


def first_send_kernel(nx, *refs):
    problem, (send_ref, high_ref, low_ref, block_ref) = refs[nx : nx + 5], refs[nx + 5 :]
    assemble(refs[:nx], block_ref)
    send_ref[...] = errors_and_part(0, problem, block_ref[...], high_ref, low_ref)


def first_keep_kernel(nx, *refs):
    problem, (keep_ref, high_ref, low_ref, block_ref) = refs[nx : nx + 5], refs[nx + 5 :]
    assemble(refs[:nx], block_ref)
    block = block_ref[...]
    part = errors_and_part(1, problem, block, high_ref, low_ref)
    keep_ref[...] = with_ridge(part, block)


def join_kernel(*refs):
    assemble(refs[:-1], refs[-1])


def later_step(count, own_ref, other_ref):
    return step_of([tile_squares(own_ref[...]), tile_squares(other_ref[...])], count)


def later_send_kernel(count, share, own_ref, other_ref, old_own_ref, old_ref, *refs):
    problem, (send_ref, high_ref, low_ref, block_ref, share_ref) = refs[:5], refs[5:]
    step = later_step(count, own_ref, other_ref)
    chip, _ = place()
    rows = aligned(chip, share)
    share_ref[...] = old_own_ref[rows, :] - step * own_ref[rows, :]
    block = old_ref[...] - step * other_ref[...]
    block_ref[...] = block
    send_ref[...] = errors_and_part(0, problem, block, high_ref, low_ref)


def later_keep_kernel(count, own_ref, other_ref, old_ref, *refs):
    problem, (keep_ref, high_ref, low_ref, block_ref) = refs[:5], refs[5:]
    step = later_step(count, own_ref, other_ref)
    block = old_ref[...] - step * own_ref[...]
    block_ref[...] = block
    part = errors_and_part(1, problem, block, high_ref, low_ref)
    keep_ref[...] = with_ridge(part, block)


def pixel_gradient(strip_ref, errors, blocks):
    joined = [jnp.concatenate([ref[...] for ref in part], 0) for part in errors]
    block = jnp.concatenate([ref[...] for ref in blocks], 0)
    return ridge * strip_ref[...] - product(joined, split(block), TN)


def gradient_kernel(strip_ref, h0, l0, h1, l1, b0, b1, grad_ref, tile_ref):
    grad = pixel_gradient(strip_ref, ((h0, h1), (l0, l1)), (b0, b1))
    grad_ref[...] = grad
    tile_ref[...] = tile_squares(grad)


def first_step_kernel(count, strip_ref, grad_ref, own_ref, other_ref, *outs):
    strip_out, h_ref, l_ref, th_ref, tl_ref = outs
    step = step_of([own_ref[...], other_ref[...]], count)
    strip = strip_ref[...] - step * grad_ref[...]
    strip_out[...] = strip
    h_ref[...], l_ref[...] = split(strip)
    th_ref[...], tl_ref[...] = split(strip.T)


def step_kernel(count, held_ref, grad_ref, *refs):
    step = step_of([t[...] for t in refs[:-1]], count)
    refs[-1][...] = held_ref[...] - step * grad_ref[...]


def last_gradient_kernel(share, *refs):
    parts, (grad_ref, tile_ref), sum_ref = refs[:-3], refs[-3:-1], refs[-1]
    total = parts[0][...]
    for ref in parts[1:]:
        total = total + ref[...]
    sum_ref[...] = total
    tile_ref[...] = tile_squares(total)
    chip, _ = place()
    grad_ref[...] = sum_ref[aligned(chip, share), :]


def on_device(readings, coverage, pixel_factors, date_factors):
    pixels, rank = pixel_factors.shape
    share = date_factors.shape[0]
    n = lax.axis_size("sub")
    blocks = lax.axis_size("blk")
    nx = n // CORES
    dates = share * n
    half = share * nx
    pixel_count = pixels * n * rank
    date_count = dates * rank
    work = pixels * dates * rank

    def moved(a, dx, dc):
        return (a // CORES + dx) % nx * CORES + (a % CORES + dc) % CORES

    def within(value, dx, dc):
        pairs = [(a, moved(a, dx, dc)) for a in range(n)]
        return lax.ppermute(value, "sub", pairs)

    def onward(value, dx):
        pairs = [
            (b * n + a, (b + 1) % blocks * n + moved(a, dx, 1))
            for b in range(blocks) for a in range(n)
        ]
        return lax.ppermute(value, ("blk", "sub"), pairs)

    def chips(value):
        return [value] + [within(value, dx, 0) for dx in range(1, nx)]

    strip_shapes = [shape(pixels, rank)] + [shape(pixels, rank, BF16)] * 2
    strip_shapes += [shape(rank, pixels, BF16)] * 2
    part_shapes = [shape(half, rank)] + [shape(half, pixels, BF16)] * 2

    def prepared(stratum, grant, *args):
        kinds = [F32, jnp.int32, F32][: len(args)]
        outs = [shape(dates, pixels)]
        if len(args) == 3:
            outs += strip_shapes
        scratch = [
            pltpu.VMEM((pixels, a.shape[-1]), kind) for a, kind in zip(args, kinds)
        ]
        scratch.append(pltpu.SemaphoreType.DMA((len(chunks_of(pixels)), len(args))))
        return call(
            functools.partial(prepare_kernel, stratum, share), outs, *args,
            where=HBM, scratch=scratch, grant=grant,
        )

    others = [within(date_factors, dx, 1) for dx in range(nx)]
    owns = chips(date_factors)
    old = onward(date_factors, 0)
    values, strip, *halves = prepared(0, WIDE, readings, coverage, pixel_factors)
    values_1, = prepared(1, GRANT, readings, coverage)
    send, h0, l0, b0 = call(
        functools.partial(first_send_kernel, nx), part_shapes + [shape(half, rank)],
        *others, values, *halves, flops=6 * work,
    )
    got = within(send, 0, 1)
    keep, h1, l1, b1 = call(
        functools.partial(first_keep_kernel, nx), part_shapes + [shape(half, rank)],
        *owns, values, *halves, flops=6 * work,
    )
    mine = keep + got
    came = [onward(mine, dx) for dx in range(nx)]
    grad, tile = call(
        gradient_kernel, [shape(pixels, rank), shape(8, 128)],
        strip, h0, l0, h1, l1, b0, b1, flops=6 * work,
    )
    tiles = [tile] + [within(tile, dx, 1) for dx in range(1, nx)]
    tile = sum(tiles[1:], tiles[0])
    other_tile = within(tile, 0, 1)
    olds = chips(old)
    old_half, = call(join_kernel, [shape(half, rank)], *olds)
    old_other = within(old_half, 0, 1)
    strip, *halves = call(
        functools.partial(first_step_kernel, pixel_count), strip_shapes,
        strip, grad, tile, other_tile,
    )
    own_grad = sum(came[1:], came[0])
    other_grad = within(own_grad, 0, 1)

    send, h0, l0, b0, own = call(
        functools.partial(later_send_kernel, date_count, share),
        part_shapes + [shape(half, rank), shape(share, rank)],
        own_grad, other_grad, old_half, old_other, values_1, *halves,
        flops=6 * work,
    )
    got = within(send, 0, 1)
    held = onward(own, 0)
    keep, h1, l1, b1 = call(
        functools.partial(later_keep_kernel, date_count),
        part_shapes + [shape(half, rank)],
        own_grad, other_grad, old_half, values_1, *halves, flops=6 * work,
    )
    mine = keep + got
    came = [onward(mine, dx) for dx in range(nx)]
    grad, tile = call(
        gradient_kernel, [shape(pixels, rank), shape(8, 128)],
        strip, h0, l0, h1, l1, b0, b1, flops=6 * work,
    )
    tiles = [tile] + [within(tile, dx, 1) for dx in range(1, nx)]
    tile = sum(tiles[1:], tiles[0])
    other_tile = within(tile, 0, 1)
    strip, = call(
        functools.partial(step_kernel, pixel_count), [shape(pixels, rank)],
        strip, grad, tile, other_tile,
    )
    date_grad, tile = call(
        functools.partial(last_gradient_kernel, share),
        [shape(share, rank), shape(8, 128)], *came,
        scratch=[pltpu.VMEM((half, rank), F32)],
    )
    other_tile = within(tile, 0, 1)
    date_out, = call(
        functools.partial(step_kernel, date_count), [shape(share, rank)],
        held, date_grad, tile, other_tile,
    )
    return strip, date_out


def solution(mesh):
    spec = P(("parts", "blk", "sub"), None)
    stacked = P(None, ("parts", "blk", "sub"), None)

    return jax.shard_map(
        on_device, mesh=mesh, in_specs=(stacked, stacked, spec, spec),
        out_specs=(spec, spec), check_vma=False,
    )
```

```python
import functools

import jax
import jax.numpy as jnp
from jax import lax
from jax.experimental import pallas as pl
from jax.experimental.pallas import tpu as pltpu
from jax.sharding import PartitionSpec as P


step_size = 0.05
ridge = 0.1
epsilon = 1e-06

CORES = 2
CHUNK = 256
HIDDEN = 1e9
GRANT = 16 << 20
WIDE = 53_000_000
F32 = jnp.float32
BF16 = jnp.bfloat16

VMEM = pl.BlockSpec(memory_space=pltpu.VMEM)
HBM = pl.BlockSpec(memory_space=pltpu.HBM)

NN = (((1,), (0,)), ((), ()))
TN = (((0,), (0,)), ((), ()))


def split(value):
    high = value.astype(BF16)
    low = (value - high.astype(F32)).astype(BF16)
    return high, low


def product(a, b, dims):
    dot = functools.partial(
        lax.dot_general, dimension_numbers=dims, preferred_element_type=F32
    )
    (a_high, a_low), (b_high, b_low) = a, b
    return dot(a_high, b_high) + (dot(a_high, b_low) + dot(a_low, b_high))


def tile_squares(value):
    squares = value * value
    rows, columns = squares.shape
    folded = squares.reshape(rows // 8, 8, columns).sum(0)
    total = folded[:, :128]
    for start in range(128, columns, 128):
        total = total + folded[:, start : start + 128]
    return total


def step_of(tiles, count):
    total = tiles[0]
    for tile in tiles[1:]:
        total = total + tile
    mean = jnp.sum(total, axis=(0, 1), keepdims=True) / count
    return step_size / jnp.sqrt(mean + epsilon)


def call(kernel, outs, *args, where=VMEM, scratch=(), flops=0, grant=GRANT):
    size = sum(a.size * a.dtype.itemsize for a in list(args) + list(outs))
    return pl.pallas_call(
        kernel,
        out_shape=outs,
        in_specs=[where] * len(args),
        out_specs=[VMEM] * len(outs),
        scratch_shapes=list(scratch),
        compiler_params=pltpu.CompilerParams(vmem_limit_bytes=grant),
        cost_estimate=pl.CostEstimate(
            flops=flops, bytes_accessed=size, transcendentals=0
        ),
    )(*args)


def shape(rows, columns, dtype=F32):
    return jax.ShapeDtypeStruct((rows, columns), dtype)


def chunks_of(pixels):
    size = CHUNK if pixels % CHUNK == 0 else pixels
    return [pl.ds(start, size) for start in range(0, pixels, size)]


def place():
    at = lax.axis_index("sub")
    return at // CORES, lax.rem(at, CORES)


def aligned(index, size):
    return pl.ds(pl.multiple_of(index * size, size), size)


def prepare_kernel(stratum, share, *refs):
    with_strip = stratum == 0
    sources = refs[: 2 + with_strip]
    outs = refs[len(sources) : len(sources) + 1 + 5 * with_strip]
    buffers, sem = refs[len(sources) + len(outs) : -1], refs[-1]
    pixels, dates = buffers[0].shape
    nx = dates // share // CORES
    chunks = chunks_of(pixels)
    copies = []
    for at, chunk in enumerate(chunks):
        row = []
        for which, (source, buffer) in enumerate(zip(sources, buffers)):
            view = source.at[chunk] if which == 2 else source.at[stratum, chunk]
            copy = pltpu.make_async_copy(view, buffer.at[chunk], sem.at[at, which])
            copy.start()
            row.append(copy)
        copies.append(row)
    _, core = place()
    for chunk, row in zip(chunks, copies):
        for copy in row:
            copy.wait()
        seen = jnp.where(buffers[1][chunk, :] != 0, buffers[0][chunk, :], HIDDEN)
        turned = seen.T
        for at in range(nx * CORES):
            own = jnp.where(core == (at + stratum) % CORES, nx, 0)
            rows = aligned(own + at // CORES, share)
            outs[0][rows, chunk] = turned[at * share : (at + 1) * share]
        if with_strip:
            strip = buffers[2][chunk, :]
            outs[1][chunk, :] = strip
            outs[2][chunk, :], outs[3][chunk, :] = split(strip)
            outs[4][:, chunk], outs[5][:, chunk] = split(strip.T)


def errors_and_part(side, problem, block, high_ref, low_ref):
    values_ref, h_ref, l_ref, th_ref, tl_ref = problem
    half = block.shape[0]
    rows = slice(side * half, (side + 1) * half)
    block = split(block)
    total = None
    for chunk in chunks_of(values_ref.shape[1]):
        strip = (h_ref[chunk, :], l_ref[chunk, :])
        values = values_ref[rows, chunk]
        predicted = product(block, (th_ref[:, chunk], tl_ref[:, chunk]), NN)
        errors = jnp.where(values < HIDDEN, values - predicted, 0.0)
        errors = split(errors)
        high_ref[:, chunk], low_ref[:, chunk] = errors
        part = product(errors, strip, NN)
        total = part if total is None else total + part
    return -total


def with_ridge(part, block):
    chip, _ = place()
    return part + jnp.where(chip == 0, ridge, 0.0) * block


def assemble(shares, block_ref):
    nx = len(shares)
    share = shares[0].shape[0]
    chip, _ = place()
    for dx, ref in enumerate(shares):
        block_ref[aligned(lax.rem(chip - dx + nx, nx), share), :] = ref[...]


def first_send_kernel(nx, *refs):
    problem, (send_ref, high_ref, low_ref, block_ref) = refs[nx : nx + 5], refs[nx + 5 :]
    assemble(refs[:nx], block_ref)
    send_ref[...] = errors_and_part(0, problem, block_ref[...], high_ref, low_ref)


def first_keep_kernel(nx, *refs):
    problem, (keep_ref, high_ref, low_ref, block_ref) = refs[nx : nx + 5], refs[nx + 5 :]
    assemble(refs[:nx], block_ref)
    block = block_ref[...]
    part = errors_and_part(1, problem, block, high_ref, low_ref)
    keep_ref[...] = with_ridge(part, block)


def join_kernel(*refs):
    assemble(refs[:-1], refs[-1])


def later_step(count, own_ref, other_ref):
    return step_of([tile_squares(own_ref[...]), tile_squares(other_ref[...])], count)


def by_target(part, out_ref, share):
    nx = part.shape[0] // share
    chip, _ = place()
    for at in range(nx):
        rows = aligned(lax.rem(at - chip + nx, nx), share)
        out_ref[rows, :] = part[at * share : (at + 1) * share]


def later_send_kernel(count, share, own_ref, other_ref, old_own_ref, old_ref, *refs):
    problem, (send_ref, high_ref, low_ref, block_ref, share_ref) = refs[:5], refs[5:]
    step = later_step(count, own_ref, other_ref)
    chip, _ = place()
    rows = aligned(chip, share)
    share_ref[...] = old_own_ref[rows, :] - step * own_ref[rows, :]
    block = old_ref[...] - step * other_ref[...]
    block_ref[...] = block
    by_target(errors_and_part(0, problem, block, high_ref, low_ref), send_ref, share)


def later_keep_kernel(count, share, own_ref, other_ref, old_ref, *refs):
    problem, (keep_ref, high_ref, low_ref, block_ref) = refs[:5], refs[5:]
    step = later_step(count, own_ref, other_ref)
    block = old_ref[...] - step * own_ref[...]
    block_ref[...] = block
    part = errors_and_part(1, problem, block, high_ref, low_ref)
    by_target(with_ridge(part, block), keep_ref, share)


def pixel_gradient(strip_ref, errors, blocks):
    joined = [jnp.concatenate([ref[...] for ref in part], 0) for part in errors]
    block = jnp.concatenate([ref[...] for ref in blocks], 0)
    return ridge * strip_ref[...] - product(joined, split(block), TN)


def gradient_kernel(strip_ref, h0, l0, h1, l1, b0, b1, grad_ref, tile_ref):
    grad = pixel_gradient(strip_ref, ((h0, h1), (l0, l1)), (b0, b1))
    grad_ref[...] = grad
    tile_ref[...] = tile_squares(grad)


def first_step_kernel(count, strip_ref, grad_ref, own_ref, other_ref, *outs):
    strip_out, h_ref, l_ref, th_ref, tl_ref = outs
    step = step_of([own_ref[...], other_ref[...]], count)
    strip = strip_ref[...] - step * grad_ref[...]
    strip_out[...] = strip
    h_ref[...], l_ref[...] = split(strip)
    th_ref[...], tl_ref[...] = split(strip.T)


def step_kernel(count, held_ref, grad_ref, *refs):
    step = step_of([t[...] for t in refs[:-1]], count)
    refs[-1][...] = held_ref[...] - step * grad_ref[...]


def last_gradient_kernel(*refs):
    parts, (grad_ref, tile_ref) = refs[:-2], refs[-2:]
    total = parts[0][...]
    for ref in parts[1:]:
        total = total + ref[...]
    grad_ref[...] = total
    tile_ref[...] = tile_squares(total)


def orders(n):
    return [(dx, dc) for dx in range(n // CORES) for dc in range(CORES)]


def on_device(readings, coverage, pixel_factors, date_factors):
    pixels, rank = pixel_factors.shape
    share = date_factors.shape[0]
    n = lax.axis_size("sub")
    blocks = lax.axis_size("blk")
    nx = n // CORES
    dates = share * n
    half = share * nx
    pixel_count = pixels * n * rank
    date_count = dates * rank
    work = pixels * dates * rank

    def moved(a, dx, dc):
        return (a // CORES + dx) % nx * CORES + (a % CORES + dc) % CORES

    def within(value, dx, dc):
        pairs = [(a, moved(a, dx, dc)) for a in range(n)]
        return lax.ppermute(value, "sub", pairs)

    def onward(value, dx):
        pairs = [
            (b * n + a, (b + 1) % blocks * n + moved(a, dx, 1))
            for b in range(blocks) for a in range(n)
        ]
        return lax.ppermute(value, ("blk", "sub"), pairs)

    def chips(value):
        return [value] + [within(value, dx, 0) for dx in range(1, nx)]

    strip_shapes = [shape(pixels, rank)] + [shape(pixels, rank, BF16)] * 2
    strip_shapes += [shape(rank, pixels, BF16)] * 2
    part_shapes = [shape(half, rank)] + [shape(half, pixels, BF16)] * 2

    def prepared(stratum, grant, *args):
        kinds = [F32, jnp.int32, F32][: len(args)]
        outs = [shape(dates, pixels)]
        if len(args) == 3:
            outs += strip_shapes
        scratch = [
            pltpu.VMEM((pixels, a.shape[-1]), kind) for a, kind in zip(args, kinds)
        ]
        scratch.append(pltpu.SemaphoreType.DMA((len(chunks_of(pixels)), len(args))))
        return call(
            functools.partial(prepare_kernel, stratum, share), outs, *args,
            where=HBM, scratch=scratch, grant=grant,
        )

    others = [within(date_factors, dx, 1) for dx in range(nx)]
    owns = chips(date_factors)
    old = onward(date_factors, 0)
    values, strip, *halves = prepared(0, WIDE, readings, coverage, pixel_factors)
    values_1, = prepared(1, GRANT, readings, coverage)
    send, h0, l0, b0 = call(
        functools.partial(first_send_kernel, nx), part_shapes + [shape(half, rank)],
        *others, values, *halves, flops=6 * work,
    )
    got = within(send, 0, 1)
    keep, h1, l1, b1 = call(
        functools.partial(first_keep_kernel, nx), part_shapes + [shape(half, rank)],
        *owns, values, *halves, flops=6 * work,
    )
    mine = keep + got
    came = [onward(mine, dx) for dx in range(nx)]
    grad, tile = call(
        gradient_kernel, [shape(pixels, rank), shape(8, 128)],
        strip, h0, l0, h1, l1, b0, b1, flops=6 * work,
    )
    tiles = [tile] + [within(tile, dx, 1) for dx in range(1, nx)]
    tile = sum(tiles[1:], tiles[0])
    other_tile = within(tile, 0, 1)
    olds = chips(old)
    old_half, = call(join_kernel, [shape(half, rank)], *olds)
    old_other = within(old_half, 0, 1)
    strip, *halves = call(
        functools.partial(first_step_kernel, pixel_count), strip_shapes,
        strip, grad, tile, other_tile,
    )
    own_grad = sum(came[1:], came[0])
    other_grad = within(own_grad, 0, 1)

    send, h0, l0, b0, own = call(
        functools.partial(later_send_kernel, date_count, share),
        part_shapes + [shape(half, rank), shape(share, rank)],
        own_grad, other_grad, old_half, old_other, values_1, *halves,
        flops=6 * work,
    )
    got = within(send, 0, 1)
    held = onward(own, 0)
    keep, h1, l1, b1 = call(
        functools.partial(later_keep_kernel, date_count, share),
        part_shapes + [shape(half, rank)],
        own_grad, other_grad, old_half, values_1, *halves, flops=6 * work,
    )
    rows = [slice(dx * share, (dx + 1) * share) for dx in range(nx)]
    came = [onward(keep[r] + got[r], dx) for dx, r in enumerate(rows)]
    grad, tile = call(
        gradient_kernel, [shape(pixels, rank), shape(8, 128)],
        strip, h0, l0, h1, l1, b0, b1, flops=6 * work,
    )
    tiles = [tile] + [within(tile, dx, 1) for dx in range(1, nx)]
    tile = sum(tiles[1:], tiles[0])
    other_tile = within(tile, 0, 1)
    strip, = call(
        functools.partial(step_kernel, pixel_count), [shape(pixels, rank)],
        strip, grad, tile, other_tile,
    )
    date_grad, tile = call(
        last_gradient_kernel, [shape(share, rank), shape(8, 128)], *came
    )
    tiles = [within(tile, *step) for step in orders(n)[1:]]
    date_out, = call(
        functools.partial(step_kernel, date_count), [shape(share, rank)],
        held, date_grad, tile, *tiles,
    )
    return strip, date_out


def solution(mesh):
    spec = P(("parts", "blk", "sub"), None)
    stacked = P(None, ("parts", "blk", "sub"), None)

    return jax.shard_map(
        on_device, mesh=mesh, in_specs=(stacked, stacked, spec, spec),
        out_specs=(spec, spec), check_vma=False,
    )
```

```python
import functools

import jax
import jax.numpy as jnp
from jax import lax
from jax.experimental import pallas as pl
from jax.experimental.pallas import tpu as pltpu
from jax.sharding import PartitionSpec as P


step_size = 0.05
ridge = 0.1
epsilon = 1e-06

CORES = 2
CHUNK = 256
HIDDEN = 1e9
GRANT = 16 << 20
WIDE = 53_000_000
F32 = jnp.float32
BF16 = jnp.bfloat16

VMEM = pl.BlockSpec(memory_space=pltpu.VMEM)
HBM = pl.BlockSpec(memory_space=pltpu.HBM)

NN = (((1,), (0,)), ((), ()))
TN = (((0,), (0,)), ((), ()))


def split(value):
    high = value.astype(BF16)
    low = (value - high.astype(F32)).astype(BF16)
    return high, low


def product(a, b, dims):
    dot = functools.partial(
        lax.dot_general, dimension_numbers=dims, preferred_element_type=F32
    )
    (a_high, a_low), (b_high, b_low) = a, b
    return dot(a_high, b_high) + (dot(a_high, b_low) + dot(a_low, b_high))


def tile_squares(value):
    squares = value * value
    rows, columns = squares.shape
    folded = squares.reshape(rows // 8, 8, columns).sum(0)
    total = folded[:, :128]
    for start in range(128, columns, 128):
        total = total + folded[:, start : start + 128]
    return total


def step_of(tiles, count):
    total = tiles[0]
    for tile in tiles[1:]:
        total = total + tile
    mean = jnp.sum(total, axis=(0, 1), keepdims=True) / count
    return step_size / jnp.sqrt(mean + epsilon)


def call(kernel, outs, *args, where=VMEM, scratch=(), flops=0, grant=GRANT):
    size = sum(a.size * a.dtype.itemsize for a in list(args) + list(outs))
    return pl.pallas_call(
        kernel,
        out_shape=outs,
        in_specs=[where] * len(args),
        out_specs=[VMEM] * len(outs),
        scratch_shapes=list(scratch),
        compiler_params=pltpu.CompilerParams(vmem_limit_bytes=grant),
        cost_estimate=pl.CostEstimate(
            flops=flops, bytes_accessed=size, transcendentals=0
        ),
    )(*args)


def shape(rows, columns, dtype=F32):
    return jax.ShapeDtypeStruct((rows, columns), dtype)


def chunks_of(pixels):
    size = CHUNK if pixels % CHUNK == 0 else pixels
    return [pl.ds(start, size) for start in range(0, pixels, size)]


def place():
    at = lax.axis_index("sub")
    return at // CORES, lax.rem(at, CORES)


def aligned(index, size):
    return pl.ds(pl.multiple_of(index * size, size), size)


def prepare_kernel(stratum, share, *refs):
    with_strip = stratum == 0
    sources = refs[: 2 + with_strip]
    outs = refs[len(sources) : len(sources) + 1 + 5 * with_strip]
    buffers, sem = refs[len(sources) + len(outs) : -1], refs[-1]
    pixels, dates = buffers[0].shape
    nx = dates // share // CORES
    chunks = chunks_of(pixels)
    copies = []
    for at, chunk in enumerate(chunks):
        row = []
        for which, (source, buffer) in enumerate(zip(sources, buffers)):
            view = source.at[chunk] if which == 2 else source.at[stratum, chunk]
            copy = pltpu.make_async_copy(view, buffer.at[chunk], sem.at[at, which])
            copy.start()
            row.append(copy)
        copies.append(row)
    _, core = place()
    for chunk, row in zip(chunks, copies):
        for copy in row:
            copy.wait()
        seen = jnp.where(buffers[1][chunk, :] != 0, buffers[0][chunk, :], HIDDEN)
        turned = seen.T
        for at in range(nx * CORES):
            own = jnp.where(core == (at + stratum) % CORES, nx, 0)
            rows = aligned(own + at // CORES, share)
            outs[0][rows, chunk] = turned[at * share : (at + 1) * share]
        if with_strip:
            strip = buffers[2][chunk, :]
            outs[1][chunk, :] = strip
            outs[2][chunk, :], outs[3][chunk, :] = split(strip)
            outs[4][:, chunk], outs[5][:, chunk] = split(strip.T)


def errors_and_part(side, problem, block, high_ref, low_ref):
    values_ref, h_ref, l_ref, th_ref, tl_ref = problem
    half = block.shape[0]
    rows = slice(side * half, (side + 1) * half)
    block = split(block)
    total = None
    for chunk in chunks_of(values_ref.shape[1]):
        strip = (h_ref[chunk, :], l_ref[chunk, :])
        values = values_ref[rows, chunk]
        predicted = product(block, (th_ref[:, chunk], tl_ref[:, chunk]), NN)
        errors = jnp.where(values < HIDDEN, values - predicted, 0.0)
        errors = split(errors)
        high_ref[:, chunk], low_ref[:, chunk] = errors
        part = product(errors, strip, NN)
        total = part if total is None else total + part
    return -total


def with_ridge(part, block):
    chip, _ = place()
    return part + jnp.where(chip == 0, ridge, 0.0) * block


def assemble(shares, block_ref):
    nx = len(shares)
    share = shares[0].shape[0]
    chip, _ = place()
    for dx, ref in enumerate(shares):
        block_ref[aligned(lax.rem(chip - dx + nx, nx), share), :] = ref[...]


def first_send_kernel(nx, *refs):
    problem, (send_ref, high_ref, low_ref, block_ref) = refs[nx : nx + 5], refs[nx + 5 :]
    assemble(refs[:nx], block_ref)
    send_ref[...] = errors_and_part(0, problem, block_ref[...], high_ref, low_ref)


def first_keep_kernel(nx, *refs):
    problem, (keep_ref, high_ref, low_ref, block_ref) = refs[nx : nx + 5], refs[nx + 5 :]
    assemble(refs[:nx], block_ref)
    block = block_ref[...]
    part = errors_and_part(1, problem, block, high_ref, low_ref)
    keep_ref[...] = with_ridge(part, block)


def join_kernel(*refs):
    assemble(refs[:-1], refs[-1])


def later_step(count, own_ref, other_ref):
    return step_of([tile_squares(own_ref[...]), tile_squares(other_ref[...])], count)


def by_target(part, out_ref, share):
    nx = part.shape[0] // share
    chip, _ = place()
    for at in range(nx):
        rows = aligned(lax.rem(at - chip + nx, nx), share)
        out_ref[rows, :] = part[at * share : (at + 1) * share]


def later_send_kernel(count, share, own_ref, other_ref, old_own_ref, old_ref, *refs):
    problem, (send_ref, high_ref, low_ref, block_ref, share_ref) = refs[:5], refs[5:]
    step = later_step(count, own_ref, other_ref)
    chip, _ = place()
    rows = aligned(chip, share)
    share_ref[...] = old_own_ref[rows, :] - step * own_ref[rows, :]
    block = old_ref[...] - step * other_ref[...]
    block_ref[...] = block
    by_target(errors_and_part(0, problem, block, high_ref, low_ref), send_ref, share)


def later_keep_kernel(count, share, own_ref, other_ref, old_ref, *refs):
    problem, (keep_ref, high_ref, low_ref, block_ref) = refs[:5], refs[5:]
    step = later_step(count, own_ref, other_ref)
    block = old_ref[...] - step * own_ref[...]
    block_ref[...] = block
    part = errors_and_part(1, problem, block, high_ref, low_ref)
    by_target(with_ridge(part, block), keep_ref, share)


def pixel_gradient(strip_ref, errors, blocks):
    joined = [jnp.concatenate([ref[...] for ref in part], 0) for part in errors]
    block = jnp.concatenate([ref[...] for ref in blocks], 0)
    return ridge * strip_ref[...] - product(joined, split(block), TN)


def gradient_kernel(strip_ref, h0, l0, h1, l1, b0, b1, grad_ref, tile_ref):
    grad = pixel_gradient(strip_ref, ((h0, h1), (l0, l1)), (b0, b1))
    grad_ref[...] = grad
    tile_ref[...] = tile_squares(grad)


def first_step_kernel(count, strip_ref, grad_ref, own_ref, other_ref, *outs):
    strip_out, h_ref, l_ref, th_ref, tl_ref = outs
    step = step_of([own_ref[...], other_ref[...]], count)
    strip = strip_ref[...] - step * grad_ref[...]
    strip_out[...] = strip
    h_ref[...], l_ref[...] = split(strip)
    th_ref[...], tl_ref[...] = split(strip.T)


def step_kernel(count, held_ref, grad_ref, *refs):
    step = step_of([t[...] for t in refs[:-1]], count)
    refs[-1][...] = held_ref[...] - step * grad_ref[...]


def last_gradient_kernel(*refs):
    parts, (grad_ref, tile_ref) = refs[:-2], refs[-2:]
    total = parts[0][...]
    for ref in parts[1:]:
        total = total + ref[...]
    grad_ref[...] = total
    tile_ref[...] = tile_squares(total)


def on_device(readings, coverage, pixel_factors, date_factors):
    pixels, rank = pixel_factors.shape
    share = date_factors.shape[0]
    n = lax.axis_size("sub")
    blocks = lax.axis_size("blk")
    nx = n // CORES
    dates = share * n
    half = share * nx
    pixel_count = pixels * n * rank
    date_count = dates * rank
    work = pixels * dates * rank

    def moved(a, dx, dc):
        return (a // CORES + dx) % nx * CORES + (a % CORES + dc) % CORES

    def within(value, dx, dc):
        pairs = [(a, moved(a, dx, dc)) for a in range(n)]
        return lax.ppermute(value, "sub", pairs)

    def onward(value, dx):
        pairs = [
            (b * n + a, (b + 1) % blocks * n + moved(a, dx, 1))
            for b in range(blocks) for a in range(n)
        ]
        return lax.ppermute(value, ("blk", "sub"), pairs)

    def chips(value):
        return [value] + [within(value, dx, 0) for dx in range(1, nx)]

    strip_shapes = [shape(pixels, rank)] + [shape(pixels, rank, BF16)] * 2
    strip_shapes += [shape(rank, pixels, BF16)] * 2
    part_shapes = [shape(half, rank)] + [shape(half, pixels, BF16)] * 2

    def prepared(stratum, grant, *args):
        kinds = [F32, jnp.int32, F32][: len(args)]
        outs = [shape(dates, pixels)]
        if len(args) == 3:
            outs += strip_shapes
        scratch = [
            pltpu.VMEM((pixels, a.shape[-1]), kind) for a, kind in zip(args, kinds)
        ]
        scratch.append(pltpu.SemaphoreType.DMA((len(chunks_of(pixels)), len(args))))
        return call(
            functools.partial(prepare_kernel, stratum, share), outs, *args,
            where=HBM, scratch=scratch, grant=grant,
        )

    others = [within(date_factors, dx, 1) for dx in range(nx)]
    owns = [date_factors]
    owns += [within(others[dx], 0, 1) for dx in range(1, nx)]
    old = onward(date_factors, 0)
    values, strip, *halves = prepared(0, WIDE, readings, coverage, pixel_factors)
    values_1, = prepared(1, GRANT, readings, coverage)
    send, h0, l0, b0 = call(
        functools.partial(first_send_kernel, nx), part_shapes + [shape(half, rank)],
        *others, values, *halves, flops=6 * work,
    )
    got = within(send, 0, 1)
    keep, h1, l1, b1 = call(
        functools.partial(first_keep_kernel, nx), part_shapes + [shape(half, rank)],
        *owns, values, *halves, flops=6 * work,
    )
    mine = keep + got
    came = [onward(mine, dx) for dx in range(nx)]
    grad, tile = call(
        gradient_kernel, [shape(pixels, rank), shape(8, 128)],
        strip, h0, l0, h1, l1, b0, b1, flops=6 * work,
    )
    tiles = [tile] + [within(tile, dx, 1) for dx in range(1, nx)]
    tile = sum(tiles[1:], tiles[0])
    other_tile = within(tile, 0, 1)
    olds = chips(old)
    old_half, = call(join_kernel, [shape(half, rank)], *olds)
    old_other = within(old_half, 0, 1)
    strip, *halves = call(
        functools.partial(first_step_kernel, pixel_count), strip_shapes,
        strip, grad, tile, other_tile,
    )
    own_grad = sum(came[1:], came[0])
    other_grad = within(own_grad, 0, 1)

    send, h0, l0, b0, own = call(
        functools.partial(later_send_kernel, date_count, share),
        part_shapes + [shape(half, rank), shape(share, rank)],
        own_grad, other_grad, old_half, old_other, values_1, *halves,
        flops=6 * work,
    )
    got = within(send, 0, 1)
    held = onward(own, 0)
    keep, h1, l1, b1 = call(
        functools.partial(later_keep_kernel, date_count, share),
        part_shapes + [shape(half, rank)],
        own_grad, other_grad, old_half, values_1, *halves, flops=6 * work,
    )
    rows = [slice(dx * share, (dx + 1) * share) for dx in range(nx)]
    came = [onward(keep[r] + got[r], dx) for dx, r in enumerate(rows)]
    grad, tile = call(
        gradient_kernel, [shape(pixels, rank), shape(8, 128)],
        strip, h0, l0, h1, l1, b0, b1, flops=6 * work,
    )
    tiles = [tile] + [within(tile, dx, 1) for dx in range(1, nx)]
    tile = sum(tiles[1:], tiles[0])
    other_tile = within(tile, 0, 1)
    strip, = call(
        functools.partial(step_kernel, pixel_count), [shape(pixels, rank)],
        strip, grad, tile, other_tile,
    )
    date_grad, tile = call(
        last_gradient_kernel, [shape(share, rank), shape(8, 128)], *came
    )
    tile = sum([within(tile, dx, 1) for dx in range(1, nx)], tile)
    other_tile = within(tile, 0, 1)
    date_out, = call(
        functools.partial(step_kernel, date_count), [shape(share, rank)],
        held, date_grad, tile, other_tile,
    )
    return strip, date_out


def solution(mesh):
    spec = P(("parts", "blk", "sub"), None)
    stacked = P(None, ("parts", "blk", "sub"), None)

    return jax.shard_map(
        on_device, mesh=mesh, in_specs=(stacked, stacked, spec, spec),
        out_specs=(spec, spec), check_vma=False,
    )
```
